32 devices in a mesh: dp: 32 (over z, y, x, core).
Axes of the slice: x: 2, y: 2, z: 4, core: 2. Of those that a mesh axis runs over, the one named last changes fastest.
Arguments:
- text: bfloat16 [768, 40, 768], P('dp'), may hold values from -6 to 6
- patches: bfloat16 [384, 145, 1024], P('dp'), may hold values from -6 to 6
- segment_ids: int32 [768, 40], P('dp'), may hold values from 0 to 7, never falling along the last dimension, each value on 1 to 10 neighbouring positions
- row_image: int32 [768], P('dp'), may hold values from 0 to 11
- self_query: bfloat16 [768, 768], P(None, 'dp'), may hold values from -0.21875 to 0.21875
- self_key: bfloat16 [768, 768], P(None, 'dp'), may hold values from -0.21875 to 0.21875
- self_value: bfloat16 [768, 768], P(None, 'dp'), may hold values from -0.21875 to 0.21875
- self_out: bfloat16 [768, 768], P(None, 'dp'), may hold values from -0.3125 to 0.3125
- cross_query: bfloat16 [768, 768], P(None, 'dp'), may hold values from -0.21875 to 0.21875
- cross_key: bfloat16 [1024, 768], P(None, 'dp'), may hold values from -0.1875 to 0.1875
- cross_value: bfloat16 [1024, 768], P(None, 'dp'), may hold values from -0.1875 to 0.1875
- cross_out: bfloat16 [768, 768], P(None, 'dp'), may hold values from -0.875 to 0.875
- ffn_up: bfloat16 [768, 3072], P(None, 'dp'), may hold values from -0.21875 to 0.21875
- ffn_down: bfloat16 [3072, 768], P(None, 'dp'), may hold values from -0.109375 to 0.109375
- norm_params: bfloat16 [6, 768], P(None, 'dp'), may hold values from -2 to 2, as said below
- cotangent: float32 [768, 40, 768], P('dp'), may hold values from -6 to 6
Outputs:
- output: float32 [768, 40, 768], P('dp')
- text_grad: float32 [768, 40, 768], P('dp')
- patch_grad: float32 [384, 145, 1024], P('dp')
- self_query_grad: float32 [768, 768], P(None, 'dp')
- self_key_grad: float32 [768, 768], P(None, 'dp')
- self_value_grad: float32 [768, 768], P(None, 'dp')
- self_out_grad: float32 [768, 768], P(None, 'dp')
- cross_query_grad: float32 [768, 768], P(None, 'dp')
- cross_key_grad: float32 [1024, 768], P(None, 'dp')
- cross_value_grad: float32 [1024, 768], P(None, 'dp')
- cross_out_grad: float32 [768, 768], P(None, 'dp')
- ffn_up_grad: float32 [768, 3072], P(None, 'dp')
- ffn_down_grad: float32 [3072, 768], P(None, 'dp')
- norm_grad: float32 [6, 768], P(None, 'dp')
The draws below stay inside these ranges and needn't reach their ends.
Inputs may be any that keep to these rules, and one draw needn't show every extreme that they name: `segment_ids`: along each packed row the phrase ids never fall; each phrase holds 1 to 10 tokens, and one holds exactly 10. Row r uses image (r // 24) * 12 + row_image[r]. `norm_params`: gain rows are positive.
All inputs are finite; a program needn't handle non-finite values.
Results may differ from the reference program's by a relative error of at most 0.019.
Values may be sent and summed in bfloat16 or wider, within the bound.
A program may use at most 320 MiB of HBM per device.

```python
import math
from functools import partial
import jax
import jax.numpy as jnp
import numpy as np
from jax import lax

D = 768
HEADS = 12
HD = 64
FF = 3072
PD = 1024
NP = 145
S = 40
SEGS = 8
PHRASE = 10
ROWS_DEV = 24
IMG_DEV = 12
ROWS = 768
IMAGES = 384


def draw_norm_params(key, part):
    first_key, second_key = jax.random.split(jax.random.fold_in(key, 17))
    extent = (6, D)
    gain_rows = jax.random.uniform(first_key, extent, jnp.float32, 0.6, 1.4)
    shift_rows = jnp.clip(0.5 * jax.random.normal(second_key, extent, jnp.float32), -2.0, 2.0)
    parity = (jnp.arange(6) % 2)[:, None]
    return jnp.where(parity == 0, gain_rows, shift_rows).astype(jnp.bfloat16)


def set_ends(result, key, low, high):
    shape = result.shape
    index_at = [jax.random.randint(jax.random.fold_in(key, axis), (), 0, shape[axis]) for axis in range(len(shape))]
    result = result.at[tuple(index_at)].set(low)
    longest = shape.index(max(shape))
    index_at[longest] = (index_at[longest] + 1) % shape[longest]
    return result.at[tuple(index_at)].set(high)


def raised(drawn, own_key, source, target, shards_of, factor):
    owner, partner = [(jnp.arange(drawn.shape[dim]) // (drawn.shape[dim] // shards_of)).reshape([-1 if axis == dim else 1 for axis in range(drawn.ndim)]) for dim in (source, target)]
    chosen = jax.random.permutation(own_key, shards_of)[partner]
    strong = (owner == chosen) | (owner == (partner + shards_of // 2) % shards_of)
    return jnp.where(strong, factor * drawn, drawn)


def block_scale(rng, shape, cuts, smallest, largest):
    loudness, own = 1.0, jax.random.fold_in(rng, 6)
    for axis_at, parts in cuts:
        draws = jnp.exp(jax.random.uniform(jax.random.fold_in(own, axis_at), (parts,), jnp.float32, smallest / len(cuts), largest / len(cuts)))
        loudness = loudness * jnp.repeat(draws, shape[axis_at] // parts).reshape([-1 if axis == axis_at else 1 for axis in range(len(shape))])
    return loudness


def split_up(number_of, total, bound, skew):
    loads = [(1 << 20) // math.isqrt(rank ** skew) + 1 for rank in range(2, number_of + 1)]
    spare, holding = total - bound - (number_of - 1), [1] * (number_of - 1)
    while spare > 0:
        free = [i for i in range(number_of - 1) if holding[i] < bound]
        whole, left = sum([loads[i] for i in free]), spare
        for i in free:
            more = min(bound - holding[i], max(1, left * loads[i] // whole), spare)
            holding[i] = holding[i] + more
            spare = spare - more
    return np.array([bound] + holding)


def ragged(stream_key, count, total, limit, slope):
    if count == 2:
        one = jax.random.randint(stream_key, (), max(1, total - limit), min(limit, total - 1) + 1)
        return jnp.stack([one, total - one])
    lengths = jnp.asarray(split_up(count, total, limit, slope), jnp.int32)
    pairs = (count - 1) // 2
    giver, receiver = lengths[1:1 + 2 * pairs:2], lengths[2:2 + 2 * pairs:2]
    margin = jnp.minimum(giver - 1, limit - receiver)
    shifted = jax.random.randint(jax.random.fold_in(stream_key, 1), (pairs,), 0, 1 << 20) % (margin + 1)
    lengths = lengths.at[1:1 + 2 * pairs:2].set(giver - shifted).at[2:2 + 2 * pairs:2].set(receiver + shifted)
    return lengths[jax.random.permutation(jax.random.fold_in(stream_key, 2), count)]


def noise(rng, shape, width, bound, shards=(), kind=jnp.bfloat16):
    entries = jax.random.normal(rng, shape, jnp.float32) * width
    if len(shards) > 0:
        entries = block_scale(rng, shape, shards, -0.22, 0.18) * entries
    return jnp.clip(entries, min=-bound, max=bound).astype(kind)


def bell_draw_with(key, dims, width, reach, pieces, heavy, kind=jnp.bfloat16):
    result = width * jax.random.normal(key, dims, jnp.float32)
    if pieces:
        result = result * block_scale(key, dims, pieces, -0.22, 0.18)
    return jnp.clip(raised(result, jax.random.fold_in(key, 3), *heavy), -reach, reach).astype(kind)


def setup_inputs(seed: int = 0) -> dict:
    streams_of = jax.random.split(jax.random.key(seed), 17)
    text = noise(streams_of[0], (ROWS, S, D), 1.0, 6.0, ((0, 32),))
    patches = noise(streams_of[1], (IMAGES, NP, PD), 1.0, 6.0, ((0, 32),))
    segment_ids = jax.vmap(lambda own: jnp.searchsorted(jnp.cumsum(ragged(own, SEGS, S, PHRASE, 0)), jnp.arange(S), side="right"))(jax.random.split(streams_of[2], ROWS)).reshape((ROWS, S)).astype(jnp.int32)
    row_image = set_ends(jax.random.randint(streams_of[3], (ROWS,), 0, IMG_DEV), jax.random.fold_in(streams_of[3], 1), 0, IMG_DEV - 1).astype(jnp.int32)
    self_query = noise(streams_of[4], (D, D), D ** -0.5, 0.21875, ((1, 32),))
    self_key = noise(streams_of[5], (D, D), D ** -0.5, 0.21875, ((1, 32),))
    self_value = noise(streams_of[6], (D, D), D ** -0.5, 0.21875, ((1, 32),))
    self_out = noise(streams_of[7], (D, D), (D // 2) ** -0.5, 0.3125, ((1, 32),))
    cross_query = noise(streams_of[8], (D, D), D ** -0.5, 0.21875, ((1, 32),))
    cross_key = noise(streams_of[9], (PD, D), PD ** -0.5, 0.1875, ((1, 32),))
    cross_value = noise(streams_of[10], (PD, D), PD ** -0.5, 0.1875, ((1, 32),))
    cross_out = noise(streams_of[11], (D, D), (D // 16) ** -0.5, 0.875, ((1, 32),))
    ffn_up = noise(streams_of[12], (D, FF), D ** -0.5, 0.21875, ((1, 32),))
    ffn_down = noise(streams_of[13], (FF, D), FF ** -0.5, 0.109375, ((1, 32),))
    norm_params = draw_norm_params(jax.random.fold_in(streams_of[16], 71), 0)
    cotangent = bell_draw_with(streams_of[15], (ROWS, S, D), 1.0, 6.0, ((0, 32),), (0, 2, 32, 2.75), jnp.float32)
    return {"text": text, "patches": patches, "segment_ids": segment_ids, "row_image": row_image, "self_query": self_query, "self_key": self_key, "self_value": self_value, "self_out": self_out, "cross_query": cross_query, "cross_key": cross_key, "cross_value": cross_value, "cross_out": cross_out, "ffn_up": ffn_up, "ffn_down": ffn_down, "norm_params": norm_params, "cotangent": cotangent}


@jax.custom_vjp
def low(v):
    return lax.optimization_barrier(v.astype(jnp.bfloat16)).astype(jnp.float32)

@jax.custom_vjp
def low_back(v):
    return v

def low_keep(v):
    return (low(v), None)

def low_pass(kept, grad):
    return (grad,)

def back_keep(v):
    return (v, None)

def back_low(kept, grad):
    return (low(grad),)
low.defvjp(low_keep, low_pass)
low_back.defvjp(back_keep, back_low)
epsilon = 1e-06
masked_score = -1e+30
highest = lax.Precision.HIGHEST

def matmul(left, right):
    return jnp.matmul(left, right, precision=highest)

def rounded(values):
    return low(low_back(values))

def normalize(residual, gain, shift):
    average = lax.optimization_barrier(jnp.mean(residual, axis=-1, keepdims=True))
    centered = residual - average
    variance = lax.optimization_barrier(jnp.mean(centered * centered, axis=-1, keepdims=True))
    return centered * lax.rsqrt(variance + epsilon) * gain + shift

def self_block(inputs):
    queries, key_rows, value_rows, phrase_ids = inputs
    scores = low_back(jnp.einsum('bqhe,bkhe->bhqk', queries, key_rows, precision=highest) * 0.125)
    allowed = phrase_ids[:, None, :, None] == phrase_ids[:, None, None, :]
    weights = low(jax.nn.softmax(jnp.where(allowed, scores, masked_score), axis=-1))
    return jnp.einsum('bhqk,bkhe->bqhe', weights, value_rows, precision=highest)

def cross_block(image_keys, image_values, inputs):
    queries, image_ids = inputs
    key_rows = jnp.take(image_keys, image_ids, axis=0)
    value_rows = jnp.take(image_values, image_ids, axis=0)
    scores = low_back(jnp.einsum('bqhe,bphe->bhqp', queries, key_rows, precision=highest) * 0.125)
    weights = low(jax.nn.softmax(scores, axis=-1))
    return jnp.einsum('bhqp,bphe->bqhe', weights, value_rows, precision=highest)

def layer(text, patches, self_query, self_key, self_value, self_out, cross_query, cross_key, cross_value, cross_out, ffn_up, ffn_down, norm_params, phrase_ids, image_ids):
    row_count = text.shape[0]
    block_rows = 4 * ROWS_DEV

    def blocked(values):
        return values.reshape(-1, block_rows, S, HEADS, HD)
    tokens = text.reshape(-1, D)
    query_self = blocked(rounded(matmul(tokens, self_query)))
    key_self = blocked(rounded(matmul(tokens, self_key)))
    value_self = blocked(rounded(matmul(tokens, self_value)))
    attended = lax.map(jax.checkpoint(self_block), (query_self, key_self, value_self, phrase_ids.reshape(-1, block_rows, S)))
    mixed_self = rounded(attended.reshape(-1, D))
    first = normalize(tokens + low_back(matmul(mixed_self, self_out)), norm_params[0], norm_params[1])
    first_low = low(first)
    query_cross = blocked(rounded(matmul(first_low, cross_query)))
    patch_rows = patches.reshape(-1, PD)
    image_keys = rounded(matmul(patch_rows, cross_key)).reshape(-1, NP, HEADS, HD)
    image_values = rounded(matmul(patch_rows, cross_value)).reshape(-1, NP, HEADS, HD)
    attended_cross = lax.map(jax.checkpoint(partial(cross_block, image_keys, image_values)), (query_cross, image_ids.reshape(-1, block_rows)))
    mixed_cross = rounded(attended_cross.reshape(-1, D))
    second = normalize(first + low_back(matmul(mixed_cross, cross_out)), norm_params[2], norm_params[3])
    second_low = low(second)
    hidden = low(jax.nn.gelu(low_back(matmul(second_low, ffn_up)), approximate=False))
    output = normalize(second + low_back(matmul(hidden, ffn_down)), norm_params[4], norm_params[5])
    return output.reshape(row_count, S, D)

def reference(text, patches, segment_ids, row_image, self_query, self_key, self_value, self_out, cross_query, cross_key, cross_value, cross_out, ffn_up, ffn_down, norm_params, cotangent):
    image_ids = (jnp.arange(ROWS, dtype=jnp.int32) // ROWS_DEV * IMG_DEV + row_image).astype(jnp.int32)

    def forward(*floats):
        return layer(*floats, segment_ids, image_ids)
    output, pullback = jax.vjp(forward, text.astype(jnp.float32), patches.astype(jnp.float32), self_query.astype(jnp.float32), self_key.astype(jnp.float32), self_value.astype(jnp.float32), self_out.astype(jnp.float32), cross_query.astype(jnp.float32), cross_key.astype(jnp.float32), cross_value.astype(jnp.float32), cross_out.astype(jnp.float32), ffn_up.astype(jnp.float32), ffn_down.astype(jnp.float32), norm_params.astype(jnp.float32))
    grads = pullback(cotangent.astype(output.dtype))
    return (output, grads[0], grads[1], grads[2], grads[3], grads[4], grads[5], grads[6], grads[7], grads[8], grads[9], grads[10], grads[11], grads[12])
```

```python
import functools

import jax
import jax.numpy as jnp
from jax import lax
from jax.experimental import pallas as pl
from jax.experimental.pallas import tpu as pltpu
from jax.sharding import PartitionSpec as P

HEADS = 12
HD = 64
LANES = 128
PAIRS = HEADS // 2
ROWS_BLOCK = 6
GROUP = 2
PATCH_PAD = 160
IMAGE_BLOCK = 4
VMEM_BYTES = 66_000_000
MASKED = -1e30
EPSILON = 1e-06
F32 = jnp.float32
BF16 = jnp.bfloat16


def nt(left, right):
    return lax.dot_general(left, right, (((1,), (1,)), ((), ())), preferred_element_type=F32)


def nn(left, right):
    return lax.dot_general(left, right, (((1,), (0,)), ((), ())), preferred_element_type=F32)


def tn(left, right):
    return lax.dot_general(left, right, (((0,), (0,)), ((), ())), preferred_element_type=F32)


def normalize(residual):
    average = jnp.mean(residual, axis=-1, keepdims=True)
    centered = residual - average
    inverse = lax.rsqrt(jnp.mean(centered * centered, axis=-1, keepdims=True) + EPSILON)
    return centered * inverse, inverse


def normalize_back(grad, normed, inverse, gain):
    scaled = grad * gain
    return inverse * (
        scaled
        - jnp.mean(scaled, axis=-1, keepdims=True)
        - normed * jnp.mean(scaled * normed, axis=-1, keepdims=True)
    )


def half_masks(dtype, scale=1.0):
    lane = lax.broadcasted_iota(jnp.int32, (1, LANES), 1)
    low = jnp.where(lane < HD, scale, 0.0)
    high = jnp.where(lane < HD, 0.0, scale)
    return low.astype(dtype), high.astype(dtype)


def merge_halves(stacked):
    half = stacked.shape[0] // 2
    lane = lax.broadcasted_iota(jnp.int32, (half, LANES), 1)
    return jnp.where(lane < HD, stacked[:half], stacked[half:])


def softmax(scores):
    exponent = jnp.exp(scores - jnp.max(scores, axis=-1, keepdims=True))
    return (exponent * (1.0 / jnp.sum(exponent, axis=-1, keepdims=True))).astype(BF16)


def images_kernel(patches_ref, key_ref, value_ref, padded_ref, keys_ref, values_ref):
    images, patches, width = patches_ref.shape
    tail = PATCH_PAD - 16
    for image in range(images):
        padded_ref[image, tail:, :] = jnp.zeros((PATCH_PAD - tail, width), BF16)
        padded_ref[image, :patches, :] = patches_ref[image]
    rows = padded_ref[...].reshape(images * PATCH_PAD, width)
    shape = (images, PATCH_PAD, key_ref.shape[0])
    keys_ref[...] = nt(rows, key_ref[...]).astype(BF16).reshape(shape)
    values_ref[...] = nt(rows, value_ref[...]).astype(BF16).reshape(shape)


def whole(shape):
    return pl.BlockSpec(shape, lambda *_: (0,) * len(shape), pipeline_mode=pl.Buffered(1))


def image_rows(patches, cross_key, cross_value):
    images, count, width = patches.shape
    inner = cross_key.shape[0]

    def block(middle, last):
        return pl.BlockSpec((IMAGE_BLOCK, middle, last), lambda i: (i, 0, 0))

    return pl.pallas_call(
        images_kernel,
        grid=(images // IMAGE_BLOCK,),
        in_specs=[block(count, width), whole(cross_key.shape), whole(cross_value.shape)],
        out_specs=[block(PATCH_PAD, width), block(PATCH_PAD, inner), block(PATCH_PAD, inner)],
        out_shape=[
            jax.ShapeDtypeStruct((images, PATCH_PAD, width), BF16),
            jax.ShapeDtypeStruct((images, PATCH_PAD, inner), BF16),
            jax.ShapeDtypeStruct((images, PATCH_PAD, inner), BF16),
        ],
        compiler_params=pltpu.CompilerParams(vmem_limit_bytes=VMEM_BYTES),
        name="image_rows",
    )(patches, cross_key, cross_value)


def patch_kernel(keys_ref, values_ref, key_ref, value_ref, out_ref):
    images, count, width = out_ref.shape
    grad = nn(keys_ref[...].reshape(-1, key_ref.shape[0]), key_ref[...])
    grad += nn(values_ref[...].reshape(-1, key_ref.shape[0]), value_ref[...])
    grad = grad.reshape(images, PATCH_PAD, width)
    for image in range(images):
        out_ref[image] = grad[image, :count]


def patch_grads(grad_keys, grad_values, cross_key, cross_value, count):
    images, _, inner = grad_keys.shape
    width = cross_key.shape[1]
    block = pl.BlockSpec((IMAGE_BLOCK, PATCH_PAD, inner), lambda i: (i, 0, 0))
    return pl.pallas_call(
        patch_kernel,
        grid=(images // IMAGE_BLOCK,),
        in_specs=[block, block, whole(cross_key.shape), whole(cross_value.shape)],
        out_specs=pl.BlockSpec((IMAGE_BLOCK, count, width), lambda i: (i, 0, 0)),
        out_shape=jax.ShapeDtypeStruct((images, count, width), F32),
        compiler_params=pltpu.CompilerParams(vmem_limit_bytes=VMEM_BYTES),
        name="patch_grads",
    )(grad_keys, grad_values, cross_key, cross_value)


def forward_kernel(
    patch_count,
    image_ref,
    text_ref,
    id_column_ref,
    id_row_ref,
    cotangent_ref,
    keys_ref,
    values_ref,
    query_ref,
    key_ref,
    value_ref,
    out_proj_ref,
    cross_query_ref,
    cross_out_ref,
    up_ref,
    down_ref,
    norm_ref,
    output_ref,
    qkv_ref,
    self_weights_ref,
    mixed_self_ref,
    normed_one_ref,
    inverse_one_ref,
    first_low_ref,
    cross_low_ref,
    cross_weights_ref,
    mixed_cross_ref,
    second_low_ref,
    hidden_ref,
    grad_pre_ref,
    branch_three_ref,
    grad_two_ref,
    norm_grad_ref,
    cross_wide,
    mixed_wide,
    slope,
):
    step = pl.program_id(0)
    length = text_ref.shape[0] // ROWS_BLOCK
    width = text_ref.shape[1]
    tokens = text_ref[...]
    for index, weight in enumerate((query_ref, key_ref, value_ref)):
        qkv_ref[:, index * width : (index + 1) * width] = nt(tokens, weight[...]).astype(BF16)

    low, high = half_masks(BF16, 0.125)
    size = GROUP * length
    for group in range(ROWS_BLOCK // GROUP):
        rows = slice(group * size, (group + 1) * size)
        same = id_column_ref[rows, :] == id_row_ref[0, group : group + 1, :]
        bias = jnp.where(same, 0.0, MASKED)
        bias = jnp.concatenate([bias, bias], axis=0)
        for pair in range(PAIRS):
            at = pair * LANES
            queries = qkv_ref[rows, at : at + LANES]
            stacked = jnp.concatenate([queries * low, queries * high], axis=0)
            scores = nt(stacked, qkv_ref[rows, width + at : width + at + LANES]) + bias
            weights = softmax(scores)
            self_weights_ref[group, pair] = weights
            mixed = nn(weights, qkv_ref[rows, 2 * width + at : 2 * width + at + LANES])
            mixed_self_ref[rows, at : at + LANES] = merge_halves(mixed).astype(BF16)

    normed_one, inverse_one = normalize(
        tokens.astype(F32) + nt(mixed_self_ref[...], out_proj_ref[...])
    )
    normed_one_ref[...] = normed_one
    inverse_one_ref[...] = inverse_one
    first = normed_one * norm_ref[0:1, :] + norm_ref[1:2, :]
    first_low_ref[...] = first.astype(BF16)
    cross_low = nt(first_low_ref[...], cross_query_ref[...]).astype(BF16)
    cross_low_ref[...] = cross_low
    cross_wide[...] = cross_low.astype(F32)

    low_wide, high_wide = half_masks(F32, 0.125)
    column = lax.broadcasted_iota(jnp.int32, (1, PATCH_PAD), 1)
    tail = jnp.where(column < patch_count, 0.0, MASKED)
    for row in range(ROWS_BLOCK):
        rows = slice(row * length, (row + 1) * length)
        image = image_ref[step * ROWS_BLOCK + row]
        for pair in range(PAIRS):
            at = pair * LANES
            queries = cross_wide[rows, at : at + LANES]
            stacked = jnp.concatenate([queries * low_wide, queries * high_wide], axis=0)
            scores = nt(stacked.astype(BF16), keys_ref[image, :, at : at + LANES]) + tail
            weights = softmax(scores)
            cross_weights_ref[row, pair] = weights
            mixed = nn(weights, values_ref[image, :, at : at + LANES])
            mixed_wide[rows, at : at + LANES] = merge_halves(mixed)
    mixed_cross_ref[...] = mixed_wide[...].astype(BF16)

    normed_two, inverse_two = normalize(first + nt(mixed_cross_ref[...], cross_out_ref[...]))
    second = normed_two * norm_ref[2:3, :] + norm_ref[3:4, :]
    second_low_ref[...] = second.astype(BF16)

    total = second
    for start in range(0, hidden_ref.shape[1], width):
        part = slice(start, start + width)
        pre = nt(second_low_ref[...], up_ref[part, :])
        gate = 0.5 + 0.5 * lax.erf(pre * 0.7071067811865476)
        slope[:, part] = (
            gate + pre * (0.3989422804014327 * jnp.exp(-0.5 * pre * pre))
        ).astype(BF16)
        hidden = (pre * gate).astype(BF16)
        hidden_ref[:, part] = hidden
        total += nt(hidden, down_ref[:, part])

    normed_three, inverse_three = normalize(total)
    output_ref[...] = normed_three * norm_ref[4:5, :] + norm_ref[5:6, :]
    grad = cotangent_ref[...]
    terms = [
        None,
        None,
        None,
        None,
        jnp.sum(grad * normed_three, axis=0, keepdims=True),
        jnp.sum(grad, axis=0, keepdims=True),
    ]
    grad_three = normalize_back(grad, normed_three, inverse_three, norm_ref[4:5, :])
    branch_three = grad_three.astype(BF16)
    branch_three_ref[...] = branch_three
    grad_second = grad_three
    for start in range(0, hidden_ref.shape[1], width):
        part = slice(start, start + width)
        grad_pre = (nn(branch_three, down_ref[:, part]) * slope[:, part].astype(F32)).astype(BF16)
        grad_pre_ref[:, part] = grad_pre
        grad_second += nn(grad_pre, up_ref[part, :])
    terms[2] = jnp.sum(grad_second * normed_two, axis=0, keepdims=True)
    terms[3] = jnp.sum(grad_second, axis=0, keepdims=True)
    grad_two_ref[...] = normalize_back(grad_second, normed_two, inverse_two, norm_ref[2:3, :])

    @pl.when(step == 0)
    def _():
        norm_grad_ref[...] = jnp.zeros_like(norm_grad_ref)

    for index in range(2, 6):
        norm_grad_ref[index : index + 1, :] += terms[index]


def forward(row_image, text, ids, cotangent, keys, values, weights, norms, patch_count):
    rows, length, width = text.shape
    hidden = weights["up"].shape[0]
    size = ROWS_BLOCK * length
    count = rows * length
    groups = ROWS_BLOCK // GROUP
    steps = rows // ROWS_BLOCK

    def tokens(last):
        return pl.BlockSpec((size, last), lambda i, *_: (i, 0))

    def units(number, left, right):
        return pl.BlockSpec((number, PAIRS, left, right), lambda i, *_: (i, 0, 0, 0))

    names = ("query", "key", "value", "out", "cross_query", "cross_out", "up", "down")
    held = [weights[name] for name in names]
    pair_rows = 2 * length
    stack_rows = 2 * GROUP * length
    outs = [
        ((count, width), F32, tokens(width)),
        ((count, 3 * width), BF16, tokens(3 * width)),
        (
            (rows // GROUP, PAIRS, stack_rows, GROUP * length),
            BF16,
            units(groups, stack_rows, GROUP * length),
        ),
        ((count, width), BF16, tokens(width)),
        ((count, width), F32, tokens(width)),
        ((count, 1), F32, tokens(1)),
        ((count, width), BF16, tokens(width)),
        ((count, width), BF16, tokens(width)),
        ((rows, PAIRS, pair_rows, PATCH_PAD), BF16, units(ROWS_BLOCK, pair_rows, PATCH_PAD)),
        ((count, width), BF16, tokens(width)),
        ((count, width), BF16, tokens(width)),
        ((count, hidden), BF16, tokens(hidden)),
        ((count, hidden), BF16, tokens(hidden)),
        ((count, width), BF16, tokens(width)),
        ((count, width), F32, tokens(width)),
        ((8, width), F32, pl.BlockSpec((8, width), lambda i, *_: (0, 0))),
    ]
    return pl.pallas_call(
        functools.partial(forward_kernel, patch_count),
        grid_spec=pltpu.PrefetchScalarGridSpec(
            num_scalar_prefetch=1,
            grid=(steps,),
            in_specs=[
                tokens(width),
                tokens(1),
                pl.BlockSpec((1, groups, GROUP * length), lambda i, *_: (i, 0, 0)),
                tokens(width),
                whole(keys.shape),
                whole(values.shape),
                *[whole(array.shape) for array in held],
                whole(norms.shape),
            ],
            out_specs=[spec for _, _, spec in outs],
            scratch_shapes=[
                pltpu.VMEM((size, width), F32),
                pltpu.VMEM((size, width), F32),
                pltpu.VMEM((size, hidden), BF16),
            ],
        ),
        out_shape=[jax.ShapeDtypeStruct(shape, dtype) for shape, dtype, _ in outs],
        compiler_params=pltpu.CompilerParams(vmem_limit_bytes=VMEM_BYTES),
        name="forward",
    )(
        row_image,
        text.reshape(count, width),
        ids.reshape(count, 1),
        ids.reshape(steps, groups, GROUP * length),
        cotangent.reshape(count, width),
        keys,
        values,
        *held,
        norms,
    )


def backward_kernel(
    image_ref,
    grad_two_ref,
    qkv_ref,
    self_weights_ref,
    normed_one_ref,
    inverse_one_ref,
    cross_low_ref,
    cross_weights_ref,
    keys_ref,
    values_ref,
    query_ref,
    key_ref,
    value_ref,
    out_proj_ref,
    cross_query_ref,
    cross_out_ref,
    norm_ref,
    text_grad_ref,
    branch_two_ref,
    grad_cross_ref,
    branch_one_ref,
    grad_qkv_ref,
    grad_keys_ref,
    grad_values_ref,
    norm_grad_ref,
    cross_wide,
    mixed_wide,
    grad_wide,
    grad_mixed,
    key_total,
    value_total,
):
    step = pl.program_id(0)
    length = grad_two_ref.shape[0] // ROWS_BLOCK
    width = grad_two_ref.shape[1]

    @pl.when(step == 0)
    def _():
        norm_grad_ref[...] = jnp.zeros_like(norm_grad_ref)
        key_total[...] = jnp.zeros_like(key_total)
        value_total[...] = jnp.zeros_like(value_total)

    grad_two = grad_two_ref[...]
    branch_two = grad_two.astype(BF16)
    branch_two_ref[...] = branch_two
    mixed_wide[...] = nn(branch_two, cross_out_ref[...])
    cross_wide[...] = cross_low_ref[...].astype(F32)
    low_wide, high_wide = half_masks(F32)
    for row in range(ROWS_BLOCK):
        rows = slice(row * length, (row + 1) * length)
        image = image_ref[step * ROWS_BLOCK + row]
        for pair in range(PAIRS):
            lanes = slice(pair * LANES, (pair + 1) * LANES)
            queries = cross_wide[rows, lanes]
            queries = jnp.concatenate([queries * low_wide, queries * high_wide], axis=0).astype(BF16)
            mixed = mixed_wide[rows, lanes]
            mixed = jnp.concatenate([mixed * low_wide, mixed * high_wide], axis=0).astype(BF16)
            weights_low = cross_weights_ref[row, pair]
            weights = weights_low.astype(F32)
            grad_weights = nt(mixed, values_ref[image, :, lanes])
            inner = jnp.sum(grad_weights * weights, axis=-1, keepdims=True)
            grad_scores = (weights * (grad_weights - inner) * 0.125).astype(BF16)
            grad_wide[rows, lanes] = merge_halves(nn(grad_scores, keys_ref[image, :, lanes]))
            key_total[image, :, lanes] += tn(grad_scores, queries)
            value_total[image, :, lanes] += tn(weights_low, mixed)
    grad_cross = grad_wide[...].astype(BF16)
    grad_cross_ref[...] = grad_cross

    grad_first = grad_two + nn(grad_cross, cross_query_ref[...])
    normed_one = normed_one_ref[...]
    norm_grad_ref[0:1, :] += jnp.sum(grad_first * normed_one, axis=0, keepdims=True)
    norm_grad_ref[1:2, :] += jnp.sum(grad_first, axis=0, keepdims=True)
    grad_one = normalize_back(grad_first, normed_one, inverse_one_ref[...], norm_ref[0:1, :])
    branch_one = grad_one.astype(BF16)
    branch_one_ref[...] = branch_one
    grad_mixed[...] = nn(branch_one, out_proj_ref[...]).astype(BF16)

    low, high = half_masks(BF16)
    size = GROUP * length
    for group in range(ROWS_BLOCK // GROUP):
        rows = slice(group * size, (group + 1) * size)
        for pair in range(PAIRS):
            at = pair * LANES
            queries = qkv_ref[rows, at : at + LANES]
            queries = jnp.concatenate([queries * low, queries * high], axis=0)
            keys = qkv_ref[rows, width + at : width + at + LANES]
            values = qkv_ref[rows, 2 * width + at : 2 * width + at + LANES]
            mixed = grad_mixed[rows, at : at + LANES]
            mixed = jnp.concatenate([mixed * low, mixed * high], axis=0)
            weights_low = self_weights_ref[group, pair]
            weights = weights_low.astype(F32)
            grad_weights = nt(mixed, values)
            inner = jnp.sum(grad_weights * weights, axis=-1, keepdims=True)
            grad_scores = (weights * (grad_weights - inner) * 0.125).astype(BF16)
            grad_qkv_ref[rows, at : at + LANES] = merge_halves(nn(grad_scores, keys)).astype(BF16)
            at += width
            grad_qkv_ref[rows, at : at + LANES] = tn(grad_scores, queries).astype(BF16)
            at += width
            grad_qkv_ref[rows, at : at + LANES] = tn(weights_low, mixed).astype(BF16)

    text_grad = grad_one
    for index, weight in enumerate((query_ref, key_ref, value_ref)):
        text_grad += nn(grad_qkv_ref[:, index * width : (index + 1) * width], weight[...])
    text_grad_ref[...] = text_grad

    @pl.when(step == pl.num_programs(0) - 1)
    def _():
        grad_keys_ref[...] = key_total[...].astype(BF16)
        grad_values_ref[...] = value_total[...].astype(BF16)


def backward(row_image, saved, keys, values, weights, norms, rows):
    grad_two, qkv, self_weights, normed_one, inverse_one, cross_low, cross_weights = saved
    count, width = grad_two.shape
    length = count // rows
    size = ROWS_BLOCK * length
    groups = ROWS_BLOCK // GROUP

    def tokens(last):
        return pl.BlockSpec((size, last), lambda i, *_: (i, 0))

    def units(number, left, right):
        return pl.BlockSpec((number, PAIRS, left, right), lambda i, *_: (i, 0, 0, 0))

    names = ("query", "key", "value", "out", "cross_query", "cross_out")
    held = [weights[name] for name in names]
    low = jax.ShapeDtypeStruct((count, width), BF16)
    images = jax.ShapeDtypeStruct(keys.shape, BF16)
    return pl.pallas_call(
        backward_kernel,
        grid_spec=pltpu.PrefetchScalarGridSpec(
            num_scalar_prefetch=1,
            grid=(rows // ROWS_BLOCK,),
            in_specs=[
                tokens(width),
                tokens(3 * width),
                units(groups, 2 * GROUP * length, GROUP * length),
                tokens(width),
                tokens(1),
                tokens(width),
                units(ROWS_BLOCK, 2 * length, PATCH_PAD),
                whole(keys.shape),
                whole(values.shape),
                *[whole(array.shape) for array in held],
                whole(norms.shape),
            ],
            out_specs=[
                tokens(width),
                tokens(width),
                tokens(width),
                tokens(width),
                tokens(3 * width),
                whole(keys.shape),
                whole(keys.shape),
                pl.BlockSpec((8, width), lambda i, *_: (0, 0)),
            ],
            scratch_shapes=[
                pltpu.VMEM((size, width), F32),
                pltpu.VMEM((size, width), F32),
                pltpu.VMEM((size, width), F32),
                pltpu.VMEM((size, width), BF16),
                pltpu.VMEM(keys.shape, F32),
                pltpu.VMEM(keys.shape, F32),
            ],
        ),
        out_shape=[
            jax.ShapeDtypeStruct((count, width), F32),
            low,
            low,
            low,
            jax.ShapeDtypeStruct((count, 3 * width), BF16),
            images,
            images,
            jax.ShapeDtypeStruct((8, width), F32),
        ],
        compiler_params=pltpu.CompilerParams(vmem_limit_bytes=VMEM_BYTES),
        name="backward",
    )(row_image, grad_two, qkv, self_weights, normed_one, inverse_one, cross_low, cross_weights, keys, values, *held, norms)


NAMES = (
    "query",
    "key",
    "value",
    "out",
    "cross_query",
    "cross_key",
    "cross_value",
    "cross_out",
    "up",
    "down",
)


def gather(shards, norm):
    full = {name: lax.all_gather(shards[name], "dp", axis=0, tiled=True) for name in NAMES}
    return full, lax.all_gather(norm, "dp", axis=1, tiled=True)


def local(text, patches, segment_ids, row_image, *rest):
    *shards, norm_params, cotangent = rest
    shards = {name: jnp.swapaxes(shard, 0, 1) for name, shard in zip(NAMES, shards, strict=True)}
    rows, length, width = text.shape
    weights, norms = gather(shards, norm_params)
    norms = norms.astype(F32)
    norms = jnp.concatenate([norms, jnp.zeros((2, width), F32)], axis=0)
    ids = segment_ids + 8 * jnp.arange(rows, dtype=jnp.int32)[:, None]
    padded, keys, values = image_rows(patches, weights["cross_key"], weights["cross_value"])
    (
        output,
        qkv,
        self_weights,
        mixed_self,
        normed_one,
        inverse_one,
        first_low,
        cross_low,
        cross_weights,
        mixed_cross,
        second_low,
        hidden,
        grad_pre,
        branch_three,
        grad_two,
        norm_late,
    ) = forward(
        row_image, text, ids, cotangent, keys, values, weights, norms, patches.shape[1]
    )
    (
        text_grad,
        branch_two,
        grad_cross,
        branch_one,
        grad_qkv,
        grad_keys,
        grad_values,
        norm_early,
    ) = backward(
        row_image,
        (grad_two, qkv, self_weights, normed_one, inverse_one, cross_low, cross_weights),
        keys,
        values,
        weights,
        norms,
        rows,
    )
    patch_grad = patch_grads(
        grad_keys, grad_values, weights["cross_key"], weights["cross_value"], patches.shape[1]
    )
    tokens = text.reshape(rows * length, width)
    patch_rows = padded.reshape(-1, padded.shape[-1])
    products = (
        (grad_qkv[:, :width], tokens),
        (grad_qkv[:, width : 2 * width], tokens),
        (grad_qkv[:, 2 * width :], tokens),
        (branch_one, mixed_self),
        (grad_cross, first_low),
        (grad_keys.reshape(-1, width), patch_rows),
        (grad_values.reshape(-1, width), patch_rows),
        (branch_two, mixed_cross),
        (grad_pre, second_low),
        (branch_three, hidden),
    )
    grads = []
    for left, right in products:
        grad = tn(left, right).astype(BF16)
        grads.append(lax.psum_scatter(grad, "dp", scatter_dimension=0, tiled=True))
    norm_grad = lax.psum_scatter(
        (norm_late + norm_early)[:6], "dp", scatter_dimension=1, tiled=True
    )
    return (
        output.reshape(text.shape),
        text_grad.reshape(text.shape),
        patch_grad,
        *[jnp.swapaxes(grad, 0, 1).astype(F32) for grad in grads],
        norm_grad,
    )


def solution(mesh):
    split = P("dp", None, None)
    columns = P(None, "dp")
    in_specs = (split, split, P("dp", None), P("dp"), *([columns] * 11), split)
    out_specs = (split, split, split, *([columns] * 11))
    return jax.shard_map(local, mesh=mesh, in_specs=in_specs, out_specs=out_specs, check_vma=False)
```

```python
import functools
import itertools
import math

import jax
import jax.numpy as jnp
from jax import lax
from jax.experimental import pallas as pl
from jax.experimental.pallas import tpu as pltpu
from jax.sharding import PartitionSpec as P

HEADS = 12
HD = 64
LANES = 128
PAIRS = HEADS // 2
ROWS_BLOCK = 6
GROUP = 2
PATCH_PAD = 160
IMAGE_BLOCK = 4
VMEM_BYTES = 66_000_000
MASKED = -1e30
EPSILON = 1e-06
TILE_ROWS = 8
MESH = pl.DeviceIdType.MESH
F32 = jnp.float32
BF16 = jnp.bfloat16


def nt(left, right):
    return lax.dot_general(left, right, (((1,), (1,)), ((), ())), preferred_element_type=F32)


def nn(left, right):
    return lax.dot_general(left, right, (((1,), (0,)), ((), ())), preferred_element_type=F32)


def tn(left, right):
    return lax.dot_general(left, right, (((0,), (0,)), ((), ())), preferred_element_type=F32)


def normalize(residual):
    average = jnp.mean(residual, axis=-1, keepdims=True)
    centered = residual - average
    inverse = lax.rsqrt(jnp.mean(centered * centered, axis=-1, keepdims=True) + EPSILON)
    return centered * inverse, inverse


def normalize_back(grad, normed, inverse, gain):
    scaled = grad * gain
    return inverse * (
        scaled
        - jnp.mean(scaled, axis=-1, keepdims=True)
        - normed * jnp.mean(scaled * normed, axis=-1, keepdims=True)
    )


def half_masks(dtype, scale=1.0):
    lane = lax.broadcasted_iota(jnp.int32, (1, LANES), 1)
    low = jnp.where(lane < HD, scale, 0.0)
    high = jnp.where(lane < HD, 0.0, scale)
    return low.astype(dtype), high.astype(dtype)


def merge_halves(stacked):
    half = stacked.shape[0] // 2
    lane = lax.broadcasted_iota(jnp.int32, (half, LANES), 1)
    return jnp.where(lane < HD, stacked[:half], stacked[half:])


def softmax(scores):
    exponent = jnp.exp(scores - jnp.max(scores, axis=-1, keepdims=True))
    return (exponent * (1.0 / jnp.sum(exponent, axis=-1, keepdims=True))).astype(BF16)


def images_kernel(patches_ref, key_ref, value_ref, padded_ref, keys_ref, values_ref):
    images, patches, width = patches_ref.shape
    tail = PATCH_PAD - 16
    for image in range(images):
        padded_ref[image, tail:, :] = jnp.zeros((PATCH_PAD - tail, width), BF16)
        padded_ref[image, :patches, :] = patches_ref[image]
    rows = padded_ref[...].reshape(images * PATCH_PAD, width)
    shape = (images, PATCH_PAD, key_ref.shape[0])
    keys_ref[...] = nt(rows, key_ref[...]).astype(BF16).reshape(shape)
    values_ref[...] = nt(rows, value_ref[...]).astype(BF16).reshape(shape)


def whole(shape):
    return pl.BlockSpec(shape, lambda *_: (0,) * len(shape), pipeline_mode=pl.Buffered(1))


def image_rows(patches, cross_key, cross_value):
    images, count, width = patches.shape
    inner = cross_key.shape[0]

    def block(middle, last):
        return pl.BlockSpec((IMAGE_BLOCK, middle, last), lambda i: (i, 0, 0))

    return pl.pallas_call(
        images_kernel,
        grid=(images // IMAGE_BLOCK,),
        in_specs=[block(count, width), whole(cross_key.shape), whole(cross_value.shape)],
        out_specs=[block(PATCH_PAD, width), block(PATCH_PAD, inner), block(PATCH_PAD, inner)],
        out_shape=[
            jax.ShapeDtypeStruct((images, PATCH_PAD, width), BF16),
            jax.ShapeDtypeStruct((images, PATCH_PAD, inner), BF16),
            jax.ShapeDtypeStruct((images, PATCH_PAD, inner), BF16),
        ],
        compiler_params=pltpu.CompilerParams(vmem_limit_bytes=VMEM_BYTES),
        name="image_rows",
    )(patches, cross_key, cross_value)


def patch_kernel(keys_ref, values_ref, key_ref, value_ref, out_ref):
    images, count, width = out_ref.shape
    grad = nn(keys_ref[...].reshape(-1, key_ref.shape[0]), key_ref[...])
    grad += nn(values_ref[...].reshape(-1, key_ref.shape[0]), value_ref[...])
    grad = grad.reshape(images, PATCH_PAD, width)
    for image in range(images):
        out_ref[image] = grad[image, :count]


def patch_grads(grad_keys, grad_values, cross_key, cross_value, count):
    images, _, inner = grad_keys.shape
    width = cross_key.shape[1]
    block = pl.BlockSpec((IMAGE_BLOCK, PATCH_PAD, inner), lambda i: (i, 0, 0))
    return pl.pallas_call(
        patch_kernel,
        grid=(images // IMAGE_BLOCK,),
        in_specs=[block, block, whole(cross_key.shape), whole(cross_value.shape)],
        out_specs=pl.BlockSpec((IMAGE_BLOCK, count, width), lambda i: (i, 0, 0)),
        out_shape=jax.ShapeDtypeStruct((images, count, width), F32),
        compiler_params=pltpu.CompilerParams(vmem_limit_bytes=VMEM_BYTES),
        name="patch_grads",
    )(grad_keys, grad_values, cross_key, cross_value)


def forward_kernel(
    patch_count,
    image_ref,
    text_ref,
    id_column_ref,
    id_row_ref,
    cotangent_ref,
    keys_ref,
    values_ref,
    query_ref,
    key_ref,
    value_ref,
    out_proj_ref,
    cross_query_ref,
    cross_out_ref,
    up_ref,
    down_ref,
    norm_ref,
    output_ref,
    qkv_ref,
    self_weights_ref,
    mixed_self_ref,
    normed_one_ref,
    inverse_one_ref,
    first_low_ref,
    cross_low_ref,
    cross_weights_ref,
    mixed_cross_ref,
    second_low_ref,
    hidden_ref,
    grad_pre_ref,
    branch_three_ref,
    grad_two_ref,
    norm_grad_ref,
    cross_wide,
    mixed_wide,
    slope,
):
    step = pl.program_id(0)
    length = text_ref.shape[0] // ROWS_BLOCK
    width = text_ref.shape[1]
    tokens = text_ref[...]
    for index, weight in enumerate((query_ref, key_ref, value_ref)):
        qkv_ref[:, index * width : (index + 1) * width] = nt(tokens, weight[...]).astype(BF16)

    low, high = half_masks(BF16, 0.125)
    size = GROUP * length
    for group in range(ROWS_BLOCK // GROUP):
        rows = slice(group * size, (group + 1) * size)
        same = id_column_ref[rows, :] == id_row_ref[0, group : group + 1, :]
        bias = jnp.where(same, 0.0, MASKED)
        bias = jnp.concatenate([bias, bias], axis=0)
        for pair in range(PAIRS):
            at = pair * LANES
            queries = qkv_ref[rows, at : at + LANES]
            stacked = jnp.concatenate([queries * low, queries * high], axis=0)
            scores = nt(stacked, qkv_ref[rows, width + at : width + at + LANES]) + bias
            weights = softmax(scores)
            self_weights_ref[group, pair] = weights
            mixed = nn(weights, qkv_ref[rows, 2 * width + at : 2 * width + at + LANES])
            mixed_self_ref[rows, at : at + LANES] = merge_halves(mixed).astype(BF16)

    normed_one, inverse_one = normalize(
        tokens.astype(F32) + nt(mixed_self_ref[...], out_proj_ref[...])
    )
    normed_one_ref[...] = normed_one
    inverse_one_ref[...] = inverse_one
    first = normed_one * norm_ref[0:1, :] + norm_ref[1:2, :]
    first_low_ref[...] = first.astype(BF16)
    cross_low = nt(first_low_ref[...], cross_query_ref[...]).astype(BF16)
    cross_low_ref[...] = cross_low
    cross_wide[...] = cross_low.astype(F32)

    low_wide, high_wide = half_masks(F32, 0.125)
    column = lax.broadcasted_iota(jnp.int32, (1, PATCH_PAD), 1)
    tail = jnp.where(column < patch_count, 0.0, MASKED)
    for row in range(ROWS_BLOCK):
        rows = slice(row * length, (row + 1) * length)
        image = image_ref[step * ROWS_BLOCK + row]
        for pair in range(PAIRS):
            at = pair * LANES
            queries = cross_wide[rows, at : at + LANES]
            stacked = jnp.concatenate([queries * low_wide, queries * high_wide], axis=0)
            scores = nt(stacked.astype(BF16), keys_ref[image, :, at : at + LANES]) + tail
            weights = softmax(scores)
            cross_weights_ref[row, pair] = weights
            mixed = nn(weights, values_ref[image, :, at : at + LANES])
            mixed_wide[rows, at : at + LANES] = merge_halves(mixed)
    mixed_cross_ref[...] = mixed_wide[...].astype(BF16)

    normed_two, inverse_two = normalize(first + nt(mixed_cross_ref[...], cross_out_ref[...]))
    second = normed_two * norm_ref[2:3, :] + norm_ref[3:4, :]
    second_low_ref[...] = second.astype(BF16)

    total = second
    for start in range(0, hidden_ref.shape[1], width):
        part = slice(start, start + width)
        pre = nt(second_low_ref[...], up_ref[part, :])
        gate = 0.5 + 0.5 * lax.erf(pre * 0.7071067811865476)
        slope[:, part] = (
            gate + pre * (0.3989422804014327 * jnp.exp(-0.5 * pre * pre))
        ).astype(BF16)
        hidden = (pre * gate).astype(BF16)
        hidden_ref[:, part] = hidden
        total += nt(hidden, down_ref[:, part])

    normed_three, inverse_three = normalize(total)
    output_ref[...] = normed_three * norm_ref[4:5, :] + norm_ref[5:6, :]
    grad = cotangent_ref[...]
    terms = [
        None,
        None,
        None,
        None,
        jnp.sum(grad * normed_three, axis=0, keepdims=True),
        jnp.sum(grad, axis=0, keepdims=True),
    ]
    grad_three = normalize_back(grad, normed_three, inverse_three, norm_ref[4:5, :])
    branch_three = grad_three.astype(BF16)
    branch_three_ref[...] = branch_three
    grad_second = grad_three
    for start in range(0, hidden_ref.shape[1], width):
        part = slice(start, start + width)
        grad_pre = (nn(branch_three, down_ref[:, part]) * slope[:, part].astype(F32)).astype(BF16)
        grad_pre_ref[:, part] = grad_pre
        grad_second += nn(grad_pre, up_ref[part, :])
    terms[2] = jnp.sum(grad_second * normed_two, axis=0, keepdims=True)
    terms[3] = jnp.sum(grad_second, axis=0, keepdims=True)
    grad_two_ref[...] = normalize_back(grad_second, normed_two, inverse_two, norm_ref[2:3, :])

    @pl.when(step == 0)
    def _():
        norm_grad_ref[...] = jnp.zeros_like(norm_grad_ref)

    for index in range(2, 6):
        norm_grad_ref[index : index + 1, :] += terms[index]


def forward(row_image, text, ids, cotangent, keys, values, weights, norms, patch_count):
    rows, length, width = text.shape
    hidden = weights["up"].shape[0]
    size = ROWS_BLOCK * length
    count = rows * length
    groups = ROWS_BLOCK // GROUP
    steps = rows // ROWS_BLOCK

    def tokens(last):
        return pl.BlockSpec((size, last), lambda i, *_: (i, 0))

    def units(number, left, right):
        return pl.BlockSpec((number, PAIRS, left, right), lambda i, *_: (i, 0, 0, 0))

    names = ("query", "key", "value", "out", "cross_query", "cross_out", "up", "down")
    held = [weights[name] for name in names]
    pair_rows = 2 * length
    stack_rows = 2 * GROUP * length
    outs = [
        ((count, width), F32, tokens(width)),
        ((count, 3 * width), BF16, tokens(3 * width)),
        (
            (rows // GROUP, PAIRS, stack_rows, GROUP * length),
            BF16,
            units(groups, stack_rows, GROUP * length),
        ),
        ((count, width), BF16, tokens(width)),
        ((count, width), F32, tokens(width)),
        ((count, 1), F32, tokens(1)),
        ((count, width), BF16, tokens(width)),
        ((count, width), BF16, tokens(width)),
        ((rows, PAIRS, pair_rows, PATCH_PAD), BF16, units(ROWS_BLOCK, pair_rows, PATCH_PAD)),
        ((count, width), BF16, tokens(width)),
        ((count, width), BF16, tokens(width)),
        ((count, hidden), BF16, tokens(hidden)),
        ((count, hidden), BF16, tokens(hidden)),
        ((count, width), BF16, tokens(width)),
        ((count, width), F32, tokens(width)),
        ((8, width), F32, pl.BlockSpec((8, width), lambda i, *_: (0, 0))),
    ]
    return pl.pallas_call(
        functools.partial(forward_kernel, patch_count),
        grid_spec=pltpu.PrefetchScalarGridSpec(
            num_scalar_prefetch=1,
            grid=(steps,),
            in_specs=[
                tokens(width),
                tokens(1),
                pl.BlockSpec((1, groups, GROUP * length), lambda i, *_: (i, 0, 0)),
                tokens(width),
                whole(keys.shape),
                whole(values.shape),
                *[whole(array.shape) for array in held],
                whole(norms.shape),
            ],
            out_specs=[spec for _, _, spec in outs],
            scratch_shapes=[
                pltpu.VMEM((size, width), F32),
                pltpu.VMEM((size, width), F32),
                pltpu.VMEM((size, hidden), BF16),
            ],
        ),
        out_shape=[jax.ShapeDtypeStruct(shape, dtype) for shape, dtype, _ in outs],
        compiler_params=pltpu.CompilerParams(vmem_limit_bytes=VMEM_BYTES),
        name="forward",
    )(
        row_image,
        text.reshape(count, width),
        ids.reshape(count, 1),
        ids.reshape(steps, groups, GROUP * length),
        cotangent.reshape(count, width),
        keys,
        values,
        *held,
        norms,
    )


def backward_kernel(
    image_ref,
    grad_two_ref,
    qkv_ref,
    self_weights_ref,
    normed_one_ref,
    inverse_one_ref,
    cross_low_ref,
    cross_weights_ref,
    keys_ref,
    values_ref,
    query_ref,
    key_ref,
    value_ref,
    out_proj_ref,
    cross_query_ref,
    cross_out_ref,
    norm_ref,
    text_grad_ref,
    branch_two_ref,
    grad_cross_ref,
    branch_one_ref,
    grad_qkv_ref,
    grad_keys_ref,
    grad_values_ref,
    norm_grad_ref,
    cross_wide,
    mixed_wide,
    grad_wide,
    grad_mixed,
    key_total,
    value_total,
):
    step = pl.program_id(0)
    length = grad_two_ref.shape[0] // ROWS_BLOCK
    width = grad_two_ref.shape[1]

    @pl.when(step == 0)
    def _():
        norm_grad_ref[...] = jnp.zeros_like(norm_grad_ref)
        key_total[...] = jnp.zeros_like(key_total)
        value_total[...] = jnp.zeros_like(value_total)

    grad_two = grad_two_ref[...]
    branch_two = grad_two.astype(BF16)
    branch_two_ref[...] = branch_two
    mixed_wide[...] = nn(branch_two, cross_out_ref[...])
    cross_wide[...] = cross_low_ref[...].astype(F32)
    low_wide, high_wide = half_masks(F32)
    for row in range(ROWS_BLOCK):
        rows = slice(row * length, (row + 1) * length)
        image = image_ref[step * ROWS_BLOCK + row]
        for pair in range(PAIRS):
            lanes = slice(pair * LANES, (pair + 1) * LANES)
            queries = cross_wide[rows, lanes]
            queries = jnp.concatenate([queries * low_wide, queries * high_wide], axis=0).astype(BF16)
            mixed = mixed_wide[rows, lanes]
            mixed = jnp.concatenate([mixed * low_wide, mixed * high_wide], axis=0).astype(BF16)
            weights_low = cross_weights_ref[row, pair]
            weights = weights_low.astype(F32)
            grad_weights = nt(mixed, values_ref[image, :, lanes])
            inner = jnp.sum(grad_weights * weights, axis=-1, keepdims=True)
            grad_scores = (weights * (grad_weights - inner) * 0.125).astype(BF16)
            grad_wide[rows, lanes] = merge_halves(nn(grad_scores, keys_ref[image, :, lanes]))
            key_total[image, :, lanes] += tn(grad_scores, queries)
            value_total[image, :, lanes] += tn(weights_low, mixed)
    grad_cross = grad_wide[...].astype(BF16)
    grad_cross_ref[...] = grad_cross

    grad_first = grad_two + nn(grad_cross, cross_query_ref[...])
    normed_one = normed_one_ref[...]
    norm_grad_ref[0:1, :] += jnp.sum(grad_first * normed_one, axis=0, keepdims=True)
    norm_grad_ref[1:2, :] += jnp.sum(grad_first, axis=0, keepdims=True)
    grad_one = normalize_back(grad_first, normed_one, inverse_one_ref[...], norm_ref[0:1, :])
    branch_one = grad_one.astype(BF16)
    branch_one_ref[...] = branch_one
    grad_mixed[...] = nn(branch_one, out_proj_ref[...]).astype(BF16)

    low, high = half_masks(BF16)
    size = GROUP * length
    for group in range(ROWS_BLOCK // GROUP):
        rows = slice(group * size, (group + 1) * size)
        for pair in range(PAIRS):
            at = pair * LANES
            queries = qkv_ref[rows, at : at + LANES]
            queries = jnp.concatenate([queries * low, queries * high], axis=0)
            keys = qkv_ref[rows, width + at : width + at + LANES]
            values = qkv_ref[rows, 2 * width + at : 2 * width + at + LANES]
            mixed = grad_mixed[rows, at : at + LANES]
            mixed = jnp.concatenate([mixed * low, mixed * high], axis=0)
            weights_low = self_weights_ref[group, pair]
            weights = weights_low.astype(F32)
            grad_weights = nt(mixed, values)
            inner = jnp.sum(grad_weights * weights, axis=-1, keepdims=True)
            grad_scores = (weights * (grad_weights - inner) * 0.125).astype(BF16)
            grad_qkv_ref[rows, at : at + LANES] = merge_halves(nn(grad_scores, keys)).astype(BF16)
            at += width
            grad_qkv_ref[rows, at : at + LANES] = tn(grad_scores, queries).astype(BF16)
            at += width
            grad_qkv_ref[rows, at : at + LANES] = tn(weights_low, mixed).astype(BF16)

    text_grad = grad_one
    for index, weight in enumerate((query_ref, key_ref, value_ref)):
        text_grad += nn(grad_qkv_ref[:, index * width : (index + 1) * width], weight[...])
    text_grad_ref[...] = text_grad

    @pl.when(step == pl.num_programs(0) - 1)
    def _():
        grad_keys_ref[...] = key_total[...].astype(BF16)
        grad_values_ref[...] = value_total[...].astype(BF16)


def backward(row_image, saved, keys, values, weights, norms, rows):
    grad_two, qkv, self_weights, normed_one, inverse_one, cross_low, cross_weights = saved
    count, width = grad_two.shape
    length = count // rows
    size = ROWS_BLOCK * length
    groups = ROWS_BLOCK // GROUP

    def tokens(last):
        return pl.BlockSpec((size, last), lambda i, *_: (i, 0))

    def units(number, left, right):
        return pl.BlockSpec((number, PAIRS, left, right), lambda i, *_: (i, 0, 0, 0))

    names = ("query", "key", "value", "out", "cross_query", "cross_out")
    held = [weights[name] for name in names]
    low = jax.ShapeDtypeStruct((count, width), BF16)
    images = jax.ShapeDtypeStruct(keys.shape, BF16)
    return pl.pallas_call(
        backward_kernel,
        grid_spec=pltpu.PrefetchScalarGridSpec(
            num_scalar_prefetch=1,
            grid=(rows // ROWS_BLOCK,),
            in_specs=[
                tokens(width),
                tokens(3 * width),
                units(groups, 2 * GROUP * length, GROUP * length),
                tokens(width),
                tokens(1),
                tokens(width),
                units(ROWS_BLOCK, 2 * length, PATCH_PAD),
                whole(keys.shape),
                whole(values.shape),
                *[whole(array.shape) for array in held],
                whole(norms.shape),
            ],
            out_specs=[
                tokens(width),
                tokens(width),
                tokens(width),
                tokens(width),
                tokens(3 * width),
                whole(keys.shape),
                whole(keys.shape),
                pl.BlockSpec((8, width), lambda i, *_: (0, 0)),
            ],
            scratch_shapes=[
                pltpu.VMEM((size, width), F32),
                pltpu.VMEM((size, width), F32),
                pltpu.VMEM((size, width), F32),
                pltpu.VMEM((size, width), BF16),
                pltpu.VMEM(keys.shape, F32),
                pltpu.VMEM(keys.shape, F32),
            ],
        ),
        out_shape=[
            jax.ShapeDtypeStruct((count, width), F32),
            low,
            low,
            low,
            jax.ShapeDtypeStruct((count, 3 * width), BF16),
            images,
            images,
            jax.ShapeDtypeStruct((8, width), F32),
        ],
        compiler_params=pltpu.CompilerParams(vmem_limit_bytes=VMEM_BYTES),
        name="backward",
    )(row_image, grad_two, qkv, self_weights, normed_one, inverse_one, cross_low, cross_weights, keys, values, *held, norms)


NAMES = (
    "query",
    "key",
    "value",
    "out",
    "cross_query",
    "cross_key",
    "cross_value",
    "cross_out",
    "up",
    "down",
)


def grid_of(devices):
    chips = devices // 2
    outer = math.gcd(chips, 4)
    rest = chips // outer
    middle = max(size for size in range(1, math.isqrt(rest) + 1) if rest % size == 0)
    return outer, middle, rest // middle, 2


def device_at(sizes, place):
    index = 0
    for size, at in zip(sizes, place):
        index = index * size + at
    return index


def unflatten(index, sizes):
    place = []
    for size in reversed(sizes):
        place.append(lax.rem(index, size))
        index = lax.div(index, size)
    return tuple(reversed(place))


def shifted(sizes, place, dim, by):
    there = [lax.rem(at + by, size) if axis == dim else at for axis, (size, at) in enumerate(zip(sizes, place))]
    return device_at(sizes, there)


def greet(sizes, place):
    barrier = pltpu.get_barrier_semaphore()
    count = 0
    for dim, size in enumerate(sizes):
        for by in range(1, size):
            pl.semaphore_signal(barrier, inc=1, device_id=(shifted(sizes, place, dim, by),), device_id_type=MESH)
            count += 1
    pl.semaphore_wait(barrier, count)


def staged(number, phases):
    return [
        (message, stage - message)
        for stage in range(number + phases)
        for message in reversed(range(number))
        if 0 <= stage - message < phases
    ]


ORDERS = ((0, 1, 2, 3), (0, 2, 1, 3))


def gather_kernel(sizes, orders, *refs):
    number = len(orders)
    shards, fulls = refs[:number], refs[number : 2 * number]
    send_sem, recv_sem, own_sem = refs[2 * number :]
    place = unflatten(lax.axis_index("dp"), sizes)
    greet(sizes, place)
    me = device_at(sizes, place)
    last = len(sizes)
    zero = (0,) * last
    sends = []

    def block(message, owner):
        rows = shards[message].shape[1]
        return fulls[message].at[:, pl.ds(owner * rows, rows), :]

    def owner_of(offset):
        return device_at(sizes, [lax.rem(at + size - back, size) for at, size, back in zip(place, sizes, offset)])

    def forward(message, offset, phase):
        owner = owner_of(offset)
        source = block(message, owner) if any(offset) else shards[message]
        for dim in orders[message][phase:]:
            for by in range(1, sizes[dim]):
                slot = device_at(sizes, [at + by if axis == dim else at for axis, at in enumerate(offset)])
                copy = pltpu.make_async_remote_copy(
                    src_ref=source,
                    dst_ref=block(message, owner),
                    send_sem=send_sem.at[message, slot],
                    recv_sem=recv_sem.at[message, slot],
                    device_id=(shifted(sizes, place, dim, by),),
                    device_id_type=MESH,
                )
                copy.start()
                sends.append(copy)

    def arrivals(message, phase):
        order = orders[message]
        free = [
            range(size)
            if dim in order[: phase - 1]
            else (range(1, size) if dim == order[phase - 1] else range(1))
            for dim, size in enumerate(sizes)
        ]
        return itertools.product(*free)

    def arrived(message, offset):
        there = block(message, owner_of(offset))
        pltpu.make_async_copy(there, there, recv_sem.at[message, device_at(sizes, offset)]).wait()

    held = [pltpu.make_async_copy(shards[at], block(at, me), own_sem.at[at]) for at in range(number)]
    for copy in held:
        copy.start()
    for message in range(number):
        forward(message, zero, 0)
    for message, phase in staged(number, last):
        if phase > 0:
            for offset in arrivals(message, phase):
                arrived(message, offset)
                forward(message, offset, phase)
    for message in range(number):
        for offset in arrivals(message, last):
            arrived(message, offset)
    for copy in held:
        copy.wait()
    for copy in sends:
        copy.wait_send()


def gather_all(shards, orders, devices):
    number = len(shards)
    return pl.pallas_call(
        functools.partial(gather_kernel, grid_of(devices), orders),
        in_specs=[pl.BlockSpec(memory_space=pltpu.VMEM)] * number,
        out_specs=[pl.BlockSpec(memory_space=pl.ANY)] * number,
        out_shape=[
            jax.ShapeDtypeStruct((shard.shape[0], shard.shape[1] * devices, shard.shape[2]), shard.dtype)
            for shard in shards
        ],
        scratch_shapes=[
            pltpu.SemaphoreType.DMA((number, devices)),
            pltpu.SemaphoreType.DMA((number, devices)),
            pltpu.SemaphoreType.DMA((number,)),
        ],
        compiler_params=pltpu.CompilerParams(collective_id=0, has_side_effects=True),
        name="gather_all",
    )(*shards)


def scatter_kernel(sizes, orders, *refs):
    number = len(orders)
    grads, outs = refs[:number], refs[number : 2 * number]
    own, core, firsts, seconds, lasts = [
        refs[number * (2 + at) : number * (3 + at)] for at in range(5)
    ]
    load_sem, send_sem, recv_sem = refs[7 * number :]
    place = unflatten(lax.axis_index("dp"), sizes)
    side = place[3]
    greet(sizes, place)
    sends = []

    def remote(message, source, target, dim, by, slot):
        copy = pltpu.make_async_remote_copy(
            src_ref=source,
            dst_ref=target,
            send_sem=send_sem.at[message, slot],
            recv_sem=recv_sem.at[message, slot],
            device_id=(shifted(sizes, place, dim, by),),
            device_id_type=MESH,
        )
        copy.start()
        sends.append(copy)

    def got(message, target, slot):
        pltpu.make_async_copy(target, target, recv_sem.at[message, slot]).wait()

    def slot_of(dim, by):
        return sum(sizes[:dim]) - dim + by

    def send(message, held, dims, dim, target):
        for by in range(1, sizes[dim]):
            there = lax.rem(place[dim] + by, sizes[dim])
            at = tuple(there if axis == dim else slice(None) for axis in dims)
            remote(message, held.at[at], target.at[by - 1], dim, by, slot_of(dim, by))

    def reduce(message, held, dims, dim, target, store):
        rest = [axis for axis in dims if axis != dim]
        for by in range(1, sizes[dim]):
            got(message, target.at[by - 1], slot_of(dim, by))

        def body(index, carry):
            at = unflatten(index, [sizes[axis] for axis in rest])
            full = list(at)
            full.insert(dims.index(dim), place[dim])
            total = held[tuple(full)].astype(F32)
            for by in range(1, sizes[dim]):
                total += target[(by - 1, *at)].astype(F32)
            store(at, total)
            return carry

        lax.fori_loop(0, math.prod(sizes[axis] for axis in rest), body, 0)
        return rest

    loads = []
    for message in range(number):
        remote(message, grads[message].at[:, :, :, 1 - side], core[message], 3, 1, 0)
        load = pltpu.make_async_copy(grads[message].at[:, :, :, side], own[message], load_sem.at[message])
        load.start()
        loads.append(load)

    def keep(ref, lead):
        def store(at, total):
            ref[(*lead, *at)] = total.astype(ref.dtype)

        return store

    def store_out(message):
        def store(at, total):
            outs[message][...] = total

        return store

    def step(message, phase):
        last, middle, first = orders[message][:3]
        everything = [0, 1, 2]
        if phase == 0:
            loads[message].wait()
            got(message, core[message], 0)

            def body(index, carry):
                at = unflatten(index, sizes[:3])
                total = own[message][at].astype(F32) + core[message][at].astype(F32)
                own[message][at] = total.astype(own[message].dtype)
                return carry

            lax.fori_loop(0, math.prod(sizes[:3]), body, 0)
            send(message, own[message], everything, first, firsts[message])
        elif phase == 1:
            rest = reduce(message, own[message], everything, first, firsts[message], keep(firsts[message], (0,)))
            send(message, firsts[message].at[0], rest, middle, seconds[message])
        elif phase == 2:
            rest = [axis for axis in everything if axis != first]
            rest = reduce(message, firsts[message].at[0], rest, middle, seconds[message], keep(seconds[message], (0,)))
            send(message, seconds[message].at[0], rest, last, lasts[message])
        else:
            reduce(message, seconds[message].at[0], [last], last, lasts[message], store_out(message))

    for message in range(number):
        step(message, 0)
    for message, phase in staged(number, 4):
        if phase > 0:
            step(message, phase)
    for copy in sends:
        copy.wait_send()


def scatter_all(grads, orders, devices):
    sizes = grid_of(devices)
    number = len(grads)
    split = [grad.reshape(*sizes, grad.shape[0] // devices, *grad.shape[1:]) for grad in grads]
    blocks = [(array.shape[4:], array.dtype) for array in split]

    def scratch(drop, lead):
        made = []
        for (shape, dtype), order in zip(blocks, orders):
            gone = order[3 - drop : 3]
            outer = [sizes[gone[0]] - 1] if lead else []
            made.append(pltpu.VMEM((*outer, *[sizes[axis] for axis in range(3) if axis not in gone], *shape), dtype))
        return made

    slots = sum(sizes) - 3
    return pl.pallas_call(
        functools.partial(scatter_kernel, sizes, orders),
        in_specs=[pl.BlockSpec(memory_space=pl.ANY)] * number,
        out_specs=[pl.BlockSpec(memory_space=pltpu.VMEM)] * number,
        out_shape=[jax.ShapeDtypeStruct(shape, F32) for shape, _ in blocks],
        scratch_shapes=[
            *scratch(0, False),
            *scratch(0, False),
            *scratch(1, True),
            *scratch(2, True),
            *scratch(3, True),
            pltpu.SemaphoreType.DMA((number,)),
            pltpu.SemaphoreType.DMA((number, slots)),
            pltpu.SemaphoreType.DMA((number, slots)),
        ],
        compiler_params=pltpu.CompilerParams(collective_id=1, has_side_effects=True, vmem_limit_bytes=VMEM_BYTES),
        name="scatter_all",
    )(*split)


GATHER_ORDERS = {
    "query": 1,
    "key": 0,
    "value": 1,
    "out": 0,
    "cross_key": 1,
    "cross_value": 0,
    "cross_query": 1,
    "cross_out": 0,
    "up": 1,
    "down": 0,
}


def aligned(devices, shards):
    return devices > 2 and devices % 2 == 0 and all(shard.shape[0] % TILE_ROWS == 0 for shard in shards.values())


def gather(devices, shards, norm):
    if not aligned(devices, shards):
        full = {name: lax.all_gather(shards[name], "dp", axis=0, tiled=True) for name in NAMES}
        return full, lax.all_gather(norm, "dp", axis=1, tiled=True)
    rows, width = norm.shape
    padded = jnp.zeros((1, TILE_ROWS, LANES), norm.dtype).at[0, :rows, :width].set(norm)
    blocks = [padded] + [shards[name][None] for name in GATHER_ORDERS]
    orders = [ORDERS[0]] + [ORDERS[at] for at in GATHER_ORDERS.values()]
    norms, *fulls = gather_all(blocks, orders, devices)
    norms = norms.reshape(devices, TILE_ROWS, LANES)[:, :rows, :width]
    norms = jnp.swapaxes(norms, 0, 1).reshape(rows, devices * width)
    return {name: array[0] for name, array in zip(GATHER_ORDERS, fulls)}, norms


SCATTER_ORDERS = {
    "down": 0,
    "up": 1,
    "cross_key": 0,
    "cross_value": 1,
    "query": 0,
    "key": 1,
    "value": 0,
    "out": 1,
    "cross_query": 0,
    "cross_out": 1,
}


def scatter(devices, shards, grads, norm):
    if not aligned(devices, shards):
        parts = [lax.psum_scatter(grads[name], "dp", scatter_dimension=0, tiled=True) for name in NAMES]
        return [part.astype(F32) for part in parts], lax.psum_scatter(norm, "dp", scatter_dimension=1, tiled=True)
    rows, width = norm.shape
    width //= devices
    norm = jnp.swapaxes(norm.reshape(rows, devices, width), 0, 1)
    padded = jnp.zeros((devices, TILE_ROWS, LANES), F32).at[:, :rows, :width].set(norm)
    blocks = [grads[name] for name in SCATTER_ORDERS] + [padded.reshape(devices * TILE_ROWS, LANES)]
    orders = [ORDERS[at] for at in SCATTER_ORDERS.values()] + [ORDERS[0]]
    *parts, norm = scatter_all(blocks, orders, devices)
    parts = dict(zip(SCATTER_ORDERS, parts))
    return [parts[name] for name in NAMES], norm[:rows, :width]


def local(devices, text, patches, segment_ids, row_image, *rest):
    *shards, norm_params, cotangent = rest
    shards = {name: jnp.swapaxes(shard, 0, 1) for name, shard in zip(NAMES, shards, strict=True)}
    rows, length, width = text.shape
    weights, norms = gather(devices, shards, norm_params)
    norms = norms.astype(F32)
    norms = jnp.concatenate([norms, jnp.zeros((2, width), F32)], axis=0)
    ids = segment_ids + 8 * jnp.arange(rows, dtype=jnp.int32)[:, None]
    padded, keys, values = image_rows(patches, weights["cross_key"], weights["cross_value"])
    (
        output,
        qkv,
        self_weights,
        mixed_self,
        normed_one,
        inverse_one,
        first_low,
        cross_low,
        cross_weights,
        mixed_cross,
        second_low,
        hidden,
        grad_pre,
        branch_three,
        grad_two,
        norm_late,
    ) = forward(
        row_image, text, ids, cotangent, keys, values, weights, norms, patches.shape[1]
    )
    (
        text_grad,
        branch_two,
        grad_cross,
        branch_one,
        grad_qkv,
        grad_keys,
        grad_values,
        norm_early,
    ) = backward(
        row_image,
        (grad_two, qkv, self_weights, normed_one, inverse_one, cross_low, cross_weights),
        keys,
        values,
        weights,
        norms,
        rows,
    )
    patch_grad = patch_grads(
        grad_keys, grad_values, weights["cross_key"], weights["cross_value"], patches.shape[1]
    )
    tokens = text.reshape(rows * length, width)
    patch_rows = padded.reshape(-1, padded.shape[-1])
    products = (
        (grad_qkv[:, :width], tokens),
        (grad_qkv[:, width : 2 * width], tokens),
        (grad_qkv[:, 2 * width :], tokens),
        (branch_one, mixed_self),
        (grad_cross, first_low),
        (grad_keys.reshape(-1, width), patch_rows),
        (grad_values.reshape(-1, width), patch_rows),
        (branch_two, mixed_cross),
        (grad_pre, second_low),
        (branch_three, hidden),
    )
    sums = {name: tn(left, right).astype(BF16) for name, (left, right) in zip(NAMES, products, strict=True)}
    grads, norm_grad = scatter(devices, shards, sums, (norm_late + norm_early)[:6])
    return (
        output.reshape(text.shape),
        text_grad.reshape(text.shape),
        patch_grad,
        *[jnp.swapaxes(grad, 0, 1) for grad in grads],
        norm_grad,
    )


def solution(mesh):
    split = P("dp", None, None)
    columns = P(None, "dp")
    in_specs = (split, split, P("dp", None), P("dp"), *([columns] * 11), split)
    out_specs = (split, split, split, *([columns] * 11))
    program = functools.partial(local, mesh.shape["dp"])
    return jax.shard_map(program, mesh=mesh, in_specs=in_specs, out_specs=out_specs, check_vma=False)
```

```python
import functools
import itertools
import math
from typing import NamedTuple

import jax
import jax.numpy as jnp
from jax import lax
from jax.experimental import pallas as pl
from jax.experimental.pallas import tpu as pltpu
from jax.sharding import PartitionSpec as P

HEADS = 12
HD = 64
LANES = 128
PAIRS = HEADS // 2
ROWS_BLOCK = 6
GROUP = 2
PATCH_PAD = 160
IMAGE_BLOCK = 4
VMEM_BYTES = 66_000_000
MASKED = -1e30
EPSILON = 1e-06
TILE_ROWS = 8
MESH = pl.DeviceIdType.MESH
F32 = jnp.float32
BF16 = jnp.bfloat16


def nt(left, right):
    return lax.dot_general(left, right, (((1,), (1,)), ((), ())), preferred_element_type=F32)


def nn(left, right):
    return lax.dot_general(left, right, (((1,), (0,)), ((), ())), preferred_element_type=F32)


def tn(left, right):
    return lax.dot_general(left, right, (((0,), (0,)), ((), ())), preferred_element_type=F32)


def normalize(residual):
    average = jnp.mean(residual, axis=-1, keepdims=True)
    centered = residual - average
    inverse = lax.rsqrt(jnp.mean(centered * centered, axis=-1, keepdims=True) + EPSILON)
    return centered * inverse, inverse


def normalize_back(grad, normed, inverse, gain):
    scaled = grad * gain
    return inverse * (
        scaled
        - jnp.mean(scaled, axis=-1, keepdims=True)
        - normed * jnp.mean(scaled * normed, axis=-1, keepdims=True)
    )


def half_masks(dtype, scale=1.0):
    lane = lax.broadcasted_iota(jnp.int32, (1, LANES), 1)
    low = jnp.where(lane < HD, scale, 0.0)
    high = jnp.where(lane < HD, 0.0, scale)
    return low.astype(dtype), high.astype(dtype)


def merge_halves(stacked):
    half = stacked.shape[0] // 2
    lane = lax.broadcasted_iota(jnp.int32, (half, LANES), 1)
    return jnp.where(lane < HD, stacked[:half], stacked[half:])


def softmax(scores):
    exponent = jnp.exp(scores - jnp.max(scores, axis=-1, keepdims=True))
    return (exponent * (1.0 / jnp.sum(exponent, axis=-1, keepdims=True))).astype(BF16)


def images_kernel(patches_ref, key_ref, value_ref, padded_ref, keys_ref, values_ref):
    images, patches, width = patches_ref.shape
    tail = PATCH_PAD - 16
    for image in range(images):
        padded_ref[image, tail:, :] = jnp.zeros((PATCH_PAD - tail, width), BF16)
        padded_ref[image, :patches, :] = patches_ref[image]
    rows = padded_ref[...].reshape(images * PATCH_PAD, width)
    shape = (images, PATCH_PAD, key_ref.shape[0])
    keys_ref[...] = nt(rows, key_ref[...]).astype(BF16).reshape(shape)
    values_ref[...] = nt(rows, value_ref[...]).astype(BF16).reshape(shape)


def whole(shape):
    return pl.BlockSpec(shape, lambda *_: (0,) * len(shape), pipeline_mode=pl.Buffered(1))


def image_rows(patches, cross_key, cross_value):
    images, count, width = patches.shape
    inner = cross_key.shape[0]

    def block(middle, last):
        return pl.BlockSpec((IMAGE_BLOCK, middle, last), lambda i: (i, 0, 0))

    return pl.pallas_call(
        images_kernel,
        grid=(images // IMAGE_BLOCK,),
        in_specs=[block(count, width), whole(cross_key.shape), whole(cross_value.shape)],
        out_specs=[block(PATCH_PAD, width), block(PATCH_PAD, inner), block(PATCH_PAD, inner)],
        out_shape=[
            jax.ShapeDtypeStruct((images, PATCH_PAD, width), BF16),
            jax.ShapeDtypeStruct((images, PATCH_PAD, inner), BF16),
            jax.ShapeDtypeStruct((images, PATCH_PAD, inner), BF16),
        ],
        compiler_params=pltpu.CompilerParams(vmem_limit_bytes=VMEM_BYTES),
        name="image_rows",
    )(patches, cross_key, cross_value)


def patch_kernel(keys_ref, values_ref, key_ref, value_ref, out_ref):
    images, count, width = out_ref.shape
    grad = nn(keys_ref[...].reshape(-1, key_ref.shape[0]), key_ref[...])
    grad += nn(values_ref[...].reshape(-1, key_ref.shape[0]), value_ref[...])
    grad = grad.reshape(images, PATCH_PAD, width)
    for image in range(images):
        out_ref[image] = grad[image, :count]


def patch_grads(grad_keys, grad_values, cross_key, cross_value, count):
    images, _, inner = grad_keys.shape
    width = cross_key.shape[1]
    block = pl.BlockSpec((IMAGE_BLOCK, PATCH_PAD, inner), lambda i: (i, 0, 0))
    return pl.pallas_call(
        patch_kernel,
        grid=(images // IMAGE_BLOCK,),
        in_specs=[block, block, whole(cross_key.shape), whole(cross_value.shape)],
        out_specs=pl.BlockSpec((IMAGE_BLOCK, count, width), lambda i: (i, 0, 0)),
        out_shape=jax.ShapeDtypeStruct((images, count, width), F32),
        compiler_params=pltpu.CompilerParams(vmem_limit_bytes=VMEM_BYTES),
        name="patch_grads",
    )(grad_keys, grad_values, cross_key, cross_value)


def forward_kernel(
    patch_count,
    image_ref,
    text_ref,
    id_column_ref,
    id_row_ref,
    cotangent_ref,
    keys_ref,
    values_ref,
    query_ref,
    key_ref,
    value_ref,
    out_proj_ref,
    cross_query_ref,
    cross_out_ref,
    up_ref,
    down_ref,
    norm_ref,
    output_ref,
    qkv_ref,
    self_weights_ref,
    mixed_self_ref,
    normed_one_ref,
    inverse_one_ref,
    first_low_ref,
    cross_low_ref,
    cross_weights_ref,
    mixed_cross_ref,
    second_low_ref,
    hidden_ref,
    grad_pre_ref,
    branch_three_ref,
    grad_two_ref,
    norm_grad_ref,
    cross_wide,
    mixed_wide,
    slope,
):
    step = pl.program_id(0)
    length = text_ref.shape[0] // ROWS_BLOCK
    width = text_ref.shape[1]
    tokens = text_ref[...]
    for index, weight in enumerate((query_ref, key_ref, value_ref)):
        qkv_ref[:, index * width : (index + 1) * width] = nt(tokens, weight[...]).astype(BF16)

    low, high = half_masks(BF16, 0.125)
    size = GROUP * length
    for group in range(ROWS_BLOCK // GROUP):
        rows = slice(group * size, (group + 1) * size)
        same = id_column_ref[rows, :] == id_row_ref[0, group : group + 1, :]
        bias = jnp.where(same, 0.0, MASKED)
        bias = jnp.concatenate([bias, bias], axis=0)
        for pair in range(PAIRS):
            at = pair * LANES
            queries = qkv_ref[rows, at : at + LANES]
            stacked = jnp.concatenate([queries * low, queries * high], axis=0)
            scores = nt(stacked, qkv_ref[rows, width + at : width + at + LANES]) + bias
            weights = softmax(scores)
            self_weights_ref[group, pair] = weights
            mixed = nn(weights, qkv_ref[rows, 2 * width + at : 2 * width + at + LANES])
            mixed_self_ref[rows, at : at + LANES] = merge_halves(mixed).astype(BF16)

    normed_one, inverse_one = normalize(
        tokens.astype(F32) + nt(mixed_self_ref[...], out_proj_ref[...])
    )
    normed_one_ref[...] = normed_one
    inverse_one_ref[...] = inverse_one
    first = normed_one * norm_ref[0:1, :] + norm_ref[1:2, :]
    first_low_ref[...] = first.astype(BF16)
    cross_low = nt(first_low_ref[...], cross_query_ref[...]).astype(BF16)
    cross_low_ref[...] = cross_low
    cross_wide[...] = cross_low.astype(F32)

    low_wide, high_wide = half_masks(F32, 0.125)
    column = lax.broadcasted_iota(jnp.int32, (1, PATCH_PAD), 1)
    tail = jnp.where(column < patch_count, 0.0, MASKED)
    for row in range(ROWS_BLOCK):
        rows = slice(row * length, (row + 1) * length)
        image = image_ref[step * ROWS_BLOCK + row]
        for pair in range(PAIRS):
            at = pair * LANES
            queries = cross_wide[rows, at : at + LANES]
            stacked = jnp.concatenate([queries * low_wide, queries * high_wide], axis=0)
            scores = nt(stacked.astype(BF16), keys_ref[image, :, at : at + LANES]) + tail
            weights = softmax(scores)
            cross_weights_ref[row, pair] = weights
            mixed = nn(weights, values_ref[image, :, at : at + LANES])
            mixed_wide[rows, at : at + LANES] = merge_halves(mixed)
    mixed_cross_ref[...] = mixed_wide[...].astype(BF16)

    normed_two, inverse_two = normalize(first + nt(mixed_cross_ref[...], cross_out_ref[...]))
    second = normed_two * norm_ref[2:3, :] + norm_ref[3:4, :]
    second_low_ref[...] = second.astype(BF16)

    total = second
    for start in range(0, hidden_ref.shape[1], width):
        part = slice(start, start + width)
        pre = nt(second_low_ref[...], up_ref[part, :])
        gate = 0.5 + 0.5 * lax.erf(pre * 0.7071067811865476)
        slope[:, part] = (
            gate + pre * (0.3989422804014327 * jnp.exp(-0.5 * pre * pre))
        ).astype(BF16)
        hidden = (pre * gate).astype(BF16)
        hidden_ref[:, part] = hidden
        total += nt(hidden, down_ref[:, part])

    normed_three, inverse_three = normalize(total)
    output_ref[...] = normed_three * norm_ref[4:5, :] + norm_ref[5:6, :]
    grad = cotangent_ref[...]
    terms = [
        None,
        None,
        None,
        None,
        jnp.sum(grad * normed_three, axis=0, keepdims=True),
        jnp.sum(grad, axis=0, keepdims=True),
    ]
    grad_three = normalize_back(grad, normed_three, inverse_three, norm_ref[4:5, :])
    branch_three = grad_three.astype(BF16)
    branch_three_ref[...] = branch_three
    grad_second = grad_three
    for start in range(0, hidden_ref.shape[1], width):
        part = slice(start, start + width)
        grad_pre = (nn(branch_three, down_ref[:, part]) * slope[:, part].astype(F32)).astype(BF16)
        grad_pre_ref[:, part] = grad_pre
        grad_second += nn(grad_pre, up_ref[part, :])
    terms[2] = jnp.sum(grad_second * normed_two, axis=0, keepdims=True)
    terms[3] = jnp.sum(grad_second, axis=0, keepdims=True)
    grad_two_ref[...] = normalize_back(grad_second, normed_two, inverse_two, norm_ref[2:3, :])

    @pl.when(step == 0)
    def _():
        norm_grad_ref[...] = jnp.zeros_like(norm_grad_ref)

    for index in range(2, 6):
        norm_grad_ref[index : index + 1, :] += terms[index]


def forward(row_image, text, ids, cotangent, keys, values, weights, norms, patch_count):
    rows, length, width = text.shape
    hidden = weights["up"].shape[0]
    size = ROWS_BLOCK * length
    count = rows * length
    groups = ROWS_BLOCK // GROUP
    steps = rows // ROWS_BLOCK

    def tokens(last):
        return pl.BlockSpec((size, last), lambda i, *_: (i, 0))

    def units(number, left, right):
        return pl.BlockSpec((number, PAIRS, left, right), lambda i, *_: (i, 0, 0, 0))

    names = ("query", "key", "value", "out", "cross_query", "cross_out", "up", "down")
    held = [weights[name] for name in names]
    pair_rows = 2 * length
    stack_rows = 2 * GROUP * length
    outs = [
        ((count, width), F32, tokens(width)),
        ((count, 3 * width), BF16, tokens(3 * width)),
        (
            (rows // GROUP, PAIRS, stack_rows, GROUP * length),
            BF16,
            units(groups, stack_rows, GROUP * length),
        ),
        ((count, width), BF16, tokens(width)),
        ((count, width), F32, tokens(width)),
        ((count, 1), F32, tokens(1)),
        ((count, width), BF16, tokens(width)),
        ((count, width), BF16, tokens(width)),
        ((rows, PAIRS, pair_rows, PATCH_PAD), BF16, units(ROWS_BLOCK, pair_rows, PATCH_PAD)),
        ((count, width), BF16, tokens(width)),
        ((count, width), BF16, tokens(width)),
        ((count, hidden), BF16, tokens(hidden)),
        ((count, hidden), BF16, tokens(hidden)),
        ((count, width), BF16, tokens(width)),
        ((count, width), F32, tokens(width)),
        ((8, width), F32, pl.BlockSpec((8, width), lambda i, *_: (0, 0))),
    ]
    return pl.pallas_call(
        functools.partial(forward_kernel, patch_count),
        grid_spec=pltpu.PrefetchScalarGridSpec(
            num_scalar_prefetch=1,
            grid=(steps,),
            in_specs=[
                tokens(width),
                tokens(1),
                pl.BlockSpec((1, groups, GROUP * length), lambda i, *_: (i, 0, 0)),
                tokens(width),
                whole(keys.shape),
                whole(values.shape),
                *[whole(array.shape) for array in held],
                whole(norms.shape),
            ],
            out_specs=[spec for _, _, spec in outs],
            scratch_shapes=[
                pltpu.VMEM((size, width), F32),
                pltpu.VMEM((size, width), F32),
                pltpu.VMEM((size, hidden), BF16),
            ],
        ),
        out_shape=[jax.ShapeDtypeStruct(shape, dtype) for shape, dtype, _ in outs],
        compiler_params=pltpu.CompilerParams(vmem_limit_bytes=VMEM_BYTES),
        name="forward",
    )(
        row_image,
        text.reshape(count, width),
        ids.reshape(count, 1),
        ids.reshape(steps, groups, GROUP * length),
        cotangent.reshape(count, width),
        keys,
        values,
        *held,
        norms,
    )


def backward_kernel(
    image_ref,
    grad_two_ref,
    qkv_ref,
    self_weights_ref,
    normed_one_ref,
    inverse_one_ref,
    cross_low_ref,
    cross_weights_ref,
    keys_ref,
    values_ref,
    query_ref,
    key_ref,
    value_ref,
    out_proj_ref,
    cross_query_ref,
    cross_out_ref,
    norm_ref,
    text_grad_ref,
    branch_two_ref,
    grad_cross_ref,
    branch_one_ref,
    grad_qkv_ref,
    grad_keys_ref,
    grad_values_ref,
    norm_grad_ref,
    cross_wide,
    mixed_wide,
    grad_wide,
    grad_mixed,
    key_total,
    value_total,
):
    step = pl.program_id(0)
    length = grad_two_ref.shape[0] // ROWS_BLOCK
    width = grad_two_ref.shape[1]

    @pl.when(step == 0)
    def _():
        norm_grad_ref[...] = jnp.zeros_like(norm_grad_ref)
        key_total[...] = jnp.zeros_like(key_total)
        value_total[...] = jnp.zeros_like(value_total)

    grad_two = grad_two_ref[...]
    branch_two = grad_two.astype(BF16)
    branch_two_ref[...] = branch_two
    mixed_wide[...] = nn(branch_two, cross_out_ref[...])
    cross_wide[...] = cross_low_ref[...].astype(F32)
    low_wide, high_wide = half_masks(F32)
    for row in range(ROWS_BLOCK):
        rows = slice(row * length, (row + 1) * length)
        image = image_ref[step * ROWS_BLOCK + row]
        for pair in range(PAIRS):
            lanes = slice(pair * LANES, (pair + 1) * LANES)
            queries = cross_wide[rows, lanes]
            queries = jnp.concatenate([queries * low_wide, queries * high_wide], axis=0).astype(BF16)
            mixed = mixed_wide[rows, lanes]
            mixed = jnp.concatenate([mixed * low_wide, mixed * high_wide], axis=0).astype(BF16)
            weights_low = cross_weights_ref[row, pair]
            weights = weights_low.astype(F32)
            grad_weights = nt(mixed, values_ref[image, :, lanes])
            inner = jnp.sum(grad_weights * weights, axis=-1, keepdims=True)
            grad_scores = (weights * (grad_weights - inner) * 0.125).astype(BF16)
            grad_wide[rows, lanes] = merge_halves(nn(grad_scores, keys_ref[image, :, lanes]))
            key_total[image, :, lanes] += tn(grad_scores, queries)
            value_total[image, :, lanes] += tn(weights_low, mixed)
    grad_cross = grad_wide[...].astype(BF16)
    grad_cross_ref[...] = grad_cross

    grad_first = grad_two + nn(grad_cross, cross_query_ref[...])
    normed_one = normed_one_ref[...]
    norm_grad_ref[0:1, :] += jnp.sum(grad_first * normed_one, axis=0, keepdims=True)
    norm_grad_ref[1:2, :] += jnp.sum(grad_first, axis=0, keepdims=True)
    grad_one = normalize_back(grad_first, normed_one, inverse_one_ref[...], norm_ref[0:1, :])
    branch_one = grad_one.astype(BF16)
    branch_one_ref[...] = branch_one
    grad_mixed[...] = nn(branch_one, out_proj_ref[...]).astype(BF16)

    low, high = half_masks(BF16)
    size = GROUP * length
    for group in range(ROWS_BLOCK // GROUP):
        rows = slice(group * size, (group + 1) * size)
        for pair in range(PAIRS):
            at = pair * LANES
            queries = qkv_ref[rows, at : at + LANES]
            queries = jnp.concatenate([queries * low, queries * high], axis=0)
            keys = qkv_ref[rows, width + at : width + at + LANES]
            values = qkv_ref[rows, 2 * width + at : 2 * width + at + LANES]
            mixed = grad_mixed[rows, at : at + LANES]
            mixed = jnp.concatenate([mixed * low, mixed * high], axis=0)
            weights_low = self_weights_ref[group, pair]
            weights = weights_low.astype(F32)
            grad_weights = nt(mixed, values)
            inner = jnp.sum(grad_weights * weights, axis=-1, keepdims=True)
            grad_scores = (weights * (grad_weights - inner) * 0.125).astype(BF16)
            grad_qkv_ref[rows, at : at + LANES] = merge_halves(nn(grad_scores, keys)).astype(BF16)
            at += width
            grad_qkv_ref[rows, at : at + LANES] = tn(grad_scores, queries).astype(BF16)
            at += width
            grad_qkv_ref[rows, at : at + LANES] = tn(weights_low, mixed).astype(BF16)

    text_grad = grad_one
    for index, weight in enumerate((query_ref, key_ref, value_ref)):
        text_grad += nn(grad_qkv_ref[:, index * width : (index + 1) * width], weight[...])
    text_grad_ref[...] = text_grad

    @pl.when(step == pl.num_programs(0) - 1)
    def _():
        grad_keys_ref[...] = key_total[...].astype(BF16)
        grad_values_ref[...] = value_total[...].astype(BF16)


def backward(row_image, saved, keys, values, weights, norms, rows):
    grad_two, qkv, self_weights, normed_one, inverse_one, cross_low, cross_weights = saved
    count, width = grad_two.shape
    length = count // rows
    size = ROWS_BLOCK * length
    groups = ROWS_BLOCK // GROUP

    def tokens(last):
        return pl.BlockSpec((size, last), lambda i, *_: (i, 0))

    def units(number, left, right):
        return pl.BlockSpec((number, PAIRS, left, right), lambda i, *_: (i, 0, 0, 0))

    names = ("query", "key", "value", "out", "cross_query", "cross_out")
    held = [weights[name] for name in names]
    low = jax.ShapeDtypeStruct((count, width), BF16)
    images = jax.ShapeDtypeStruct(keys.shape, BF16)
    return pl.pallas_call(
        backward_kernel,
        grid_spec=pltpu.PrefetchScalarGridSpec(
            num_scalar_prefetch=1,
            grid=(rows // ROWS_BLOCK,),
            in_specs=[
                tokens(width),
                tokens(3 * width),
                units(groups, 2 * GROUP * length, GROUP * length),
                tokens(width),
                tokens(1),
                tokens(width),
                units(ROWS_BLOCK, 2 * length, PATCH_PAD),
                whole(keys.shape),
                whole(values.shape),
                *[whole(array.shape) for array in held],
                whole(norms.shape),
            ],
            out_specs=[
                tokens(width),
                tokens(width),
                tokens(width),
                tokens(width),
                tokens(3 * width),
                whole(keys.shape),
                whole(keys.shape),
                pl.BlockSpec((8, width), lambda i, *_: (0, 0)),
            ],
            scratch_shapes=[
                pltpu.VMEM((size, width), F32),
                pltpu.VMEM((size, width), F32),
                pltpu.VMEM((size, width), F32),
                pltpu.VMEM((size, width), BF16),
                pltpu.VMEM(keys.shape, F32),
                pltpu.VMEM(keys.shape, F32),
            ],
        ),
        out_shape=[
            jax.ShapeDtypeStruct((count, width), F32),
            low,
            low,
            low,
            jax.ShapeDtypeStruct((count, 3 * width), BF16),
            images,
            images,
            jax.ShapeDtypeStruct((8, width), F32),
        ],
        compiler_params=pltpu.CompilerParams(vmem_limit_bytes=VMEM_BYTES),
        name="backward",
    )(row_image, grad_two, qkv, self_weights, normed_one, inverse_one, cross_low, cross_weights, keys, values, *held, norms)


NAMES = (
    "query",
    "key",
    "value",
    "out",
    "cross_query",
    "cross_key",
    "cross_value",
    "cross_out",
    "up",
    "down",
)


def grid_of(devices):
    chips = devices // 2
    outer = math.gcd(chips, 4)
    rest = chips // outer
    middle = max(size for size in range(1, math.isqrt(rest) + 1) if rest % size == 0)
    return outer, middle, rest // middle, 2


def device_at(sizes, place):
    index = 0
    for size, at in zip(sizes, place):
        index = index * size + at
    return index


def unflatten(index, sizes):
    place = []
    for size in reversed(sizes):
        place.append(lax.rem(index, size))
        index = lax.div(index, size)
    return tuple(reversed(place))


def shifted(sizes, place, dim, by):
    there = [lax.rem(at + by, size) if axis == dim else at for axis, (size, at) in enumerate(zip(sizes, place))]
    return device_at(sizes, there)


def greet(sizes, place):
    barrier = pltpu.get_barrier_semaphore()
    count = 0
    for dim, size in enumerate(sizes):
        for by in range(1, size):
            pl.semaphore_signal(barrier, inc=1, device_id=(shifted(sizes, place, dim, by),), device_id_type=MESH)
            count += 1
    pl.semaphore_wait(barrier, count)


def staged(number, phases):
    return [
        (message, stage - message)
        for stage in range(number + phases)
        for message in reversed(range(number))
        if 0 <= stage - message < phases
    ]


ORDERS = ((0, 1, 2, 3), (0, 2, 1, 3))


def gather_kernel(sizes, orders, *refs):
    number = len(orders)
    shards, fulls = refs[:number], refs[number : 2 * number]
    send_sem, recv_sem, own_sem = refs[2 * number :]
    place = unflatten(lax.axis_index("dp"), sizes)
    greet(sizes, place)
    me = device_at(sizes, place)
    last = len(sizes)
    zero = (0,) * last
    sends = []

    def block(message, owner):
        rows = shards[message].shape[1]
        return fulls[message].at[:, pl.ds(owner * rows, rows), :]

    def owner_of(offset):
        return device_at(sizes, [lax.rem(at + size - back, size) for at, size, back in zip(place, sizes, offset)])

    def forward(message, offset, phase):
        owner = owner_of(offset)
        source = block(message, owner) if any(offset) else shards[message]
        for dim in orders[message][phase:]:
            for by in range(1, sizes[dim]):
                slot = device_at(sizes, [at + by if axis == dim else at for axis, at in enumerate(offset)])
                copy = pltpu.make_async_remote_copy(
                    src_ref=source,
                    dst_ref=block(message, owner),
                    send_sem=send_sem.at[message, slot],
                    recv_sem=recv_sem.at[message, slot],
                    device_id=(shifted(sizes, place, dim, by),),
                    device_id_type=MESH,
                )
                copy.start()
                sends.append(copy)

    def arrivals(message, phase):
        order = orders[message]
        free = [
            range(size)
            if dim in order[: phase - 1]
            else (range(1, size) if dim == order[phase - 1] else range(1))
            for dim, size in enumerate(sizes)
        ]
        return itertools.product(*free)

    def arrived(message, offset):
        there = block(message, owner_of(offset))
        pltpu.make_async_copy(there, there, recv_sem.at[message, device_at(sizes, offset)]).wait()

    held = [pltpu.make_async_copy(shards[at], block(at, me), own_sem.at[at]) for at in range(number)]
    for copy in held:
        copy.start()
    for message in range(number):
        forward(message, zero, 0)
    for message, phase in staged(number, last):
        if phase > 0:
            for offset in arrivals(message, phase):
                arrived(message, offset)
                forward(message, offset, phase)
    for message in range(number):
        for offset in arrivals(message, last):
            arrived(message, offset)
    for copy in held:
        copy.wait()
    for copy in sends:
        copy.wait_send()


def gather_all(shards, orders, devices):
    number = len(shards)
    return pl.pallas_call(
        functools.partial(gather_kernel, grid_of(devices), orders),
        in_specs=[pl.BlockSpec(memory_space=pltpu.VMEM)] * number,
        out_specs=[pl.BlockSpec(memory_space=pl.ANY)] * number,
        out_shape=[
            jax.ShapeDtypeStruct((shard.shape[0], shard.shape[1] * devices, shard.shape[2]), shard.dtype)
            for shard in shards
        ],
        scratch_shapes=[
            pltpu.SemaphoreType.DMA((number, devices)),
            pltpu.SemaphoreType.DMA((number, devices)),
            pltpu.SemaphoreType.DMA((number,)),
        ],
        compiler_params=pltpu.CompilerParams(collective_id=0, has_side_effects=True),
        name="gather_all",
    )(*shards)


LAGS = (1, 3, 5, 7)


class Message(NamedTuple):
    order: tuple
    rows: int
    width: int
    dtype: type
    out: int
    at: tuple
    start: int
    ring: int
    slot: int


class Job(NamedTuple):
    left: int
    left_start: int
    right: int
    right_start: int
    width: int
    messages: tuple
    plane: int | None


def products_kernel(sizes, jobs, messages, number_in, number_out, number_rings, *refs):
    count = len(messages)
    inputs, norm = refs[:number_in], refs[number_in]
    outs = refs[number_in + 1 : number_in + 1 + number_out]
    refs = refs[number_in + 1 + number_out :]
    own, core, firsts, seconds, lasts = [refs[count * at : count * (at + 1)] for at in range(5)]
    rings = refs[5 * count : 5 * count + number_rings]
    lefts, rights, product, job_sem, load_sem, send_sem, recv_sem = refs[5 * count + number_rings :]
    place = unflatten(lax.axis_index("dp"), sizes)
    side = place[3]
    blocks = math.prod(sizes[:3])
    greet(sizes, place)
    sends = []

    def remote(message, source, target, dim, by, slot):
        copy = pltpu.make_async_remote_copy(
            src_ref=source,
            dst_ref=target,
            send_sem=send_sem.at[message, slot],
            recv_sem=recv_sem.at[message, slot],
            device_id=(shifted(sizes, place, dim, by),),
            device_id_type=MESH,
        )
        copy.start()
        return copy

    def got(message, target, slot):
        pltpu.make_async_copy(target, target, recv_sem.at[message, slot]).wait()

    def slot_of(dim, by):
        return sum(sizes[:dim]) - dim + by

    def send(message, held, dims, dim, target):
        for by in range(1, sizes[dim]):
            there = lax.rem(place[dim] + by, sizes[dim])
            at = tuple(there if axis == dim else slice(None) for axis in dims)
            sends.append(remote(message, held.at[at], target.at[by - 1], dim, by, slot_of(dim, by)))

    def reduce(message, held, dims, dim, target, store):
        rest = [axis for axis in dims if axis != dim]
        for by in range(1, sizes[dim]):
            got(message, target.at[by - 1], slot_of(dim, by))

        def body(index, carry):
            at = unflatten(index, [sizes[axis] for axis in rest])
            full = list(at)
            full.insert(dims.index(dim), place[dim])
            total = held[tuple(full)].astype(F32)
            for by in range(1, sizes[dim]):
                total += target[(by - 1, *at)].astype(F32)
            store(at, total)
            return carry

        lax.fori_loop(0, math.prod(sizes[axis] for axis in rest), body, 0)
        return rest

    def keep(ref):
        def store(at, total):
            ref[(0, *at)] = total.astype(ref.dtype)

        return store

    def store_out(message):
        def store(at, total):
            columns = slice(message.start, message.start + message.width)
            outs[message.out][(*message.at, slice(None), columns)] = total

        return store

    loads = {}
    exchanges = {}

    def step(index, phase):
        message = messages[index]
        last, middle, first = message.order[:3]
        everything = [0, 1, 2]
        if phase == 0:
            if index in loads:
                loads[index].wait()
            got(index, core[index], 0)

            def body(step, carry):
                at = unflatten(step, sizes[:3])
                total = own[index][at].astype(F32) + core[index][at].astype(F32)
                own[index][at] = total.astype(own[index].dtype)
                return carry

            lax.fori_loop(0, blocks, body, 0)
            send(index, own[index], everything, first, firsts[index])
        elif phase == 1:
            rest = reduce(index, own[index], everything, first, firsts[index], keep(firsts[index]))
            send(index, firsts[index].at[0], rest, middle, seconds[index])
        elif phase == 2:
            rest = [axis for axis in everything if axis != first]
            rest = reduce(index, firsts[index].at[0], rest, middle, seconds[index], keep(seconds[index]))
            send(index, seconds[index].at[0], rest, last, lasts[index])
        else:
            reduce(index, seconds[index].at[0], [last], last, lasts[index], store_out(message))

    tail = count - 1
    exchanges[tail] = remote(tail, norm.at[:, :, :, 1 - side], core[tail], 3, 1, 0)
    loads[tail] = pltpu.make_async_copy(norm.at[:, :, :, side], own[tail], load_sem)
    loads[tail].start()

    def load(at):
        job = jobs[at]
        pair = []
        for which, (index, start, width, slots) in enumerate(
            ((job.left, job.left_start, lefts.shape[2], lefts), (job.right, job.right_start, job.width, rights))
        ):
            source = inputs[index]
            target = slots.at[at % 2, pl.ds(0, source.shape[0]), pl.ds(0, width)]
            pair.append(pltpu.make_async_copy(source.at[:, pl.ds(start, width)], target, job_sem.at[at, which]))
            pair[-1].start()
        return pair

    holder = {}

    def produce(at):
        job = jobs[at]
        depth = inputs[job.left].shape[0]
        half = lefts.shape[2] // 2

        def multiply(part, carry):
            lanes = pl.ds(pl.multiple_of(part * half, half), half)
            product[lanes, : job.width] = tn(lefts[at % 2, :depth, lanes], rights[at % 2, :depth, : job.width])
            return carry

        lax.fori_loop(0, 2, multiply, 0)
        for part, index in enumerate(job.messages):
            message = messages[index]
            if holder.get((message.ring, message.slot), index) != index:
                exchanges.pop(holder[message.ring, message.slot]).wait_send()
            holder[message.ring, message.slot] = index
            columns = slice(part * message.width, (part + 1) * message.width)
            steps = blocks if job.plane is None else blocks // sizes[0]

            def split(step, carry):
                where = unflatten(step, sizes[:3] if job.plane is None else sizes[1:3])
                where = where if job.plane is None else (job.plane, *where)
                base = pl.multiple_of(step * 2 * message.rows, TILE_ROWS)
                even = product[pl.ds(base, message.rows), columns]
                odd = product[pl.ds(base + message.rows, message.rows), columns]
                own[index][where] = jnp.where(side == 0, even, odd).astype(BF16)
                rings[message.ring][(message.slot, *where)] = jnp.where(side == 0, odd, even).astype(BF16)
                return carry

            lax.fori_loop(0, steps, split, 0)
            if job.plane in (None, sizes[0] - 1):
                exchanges[index] = remote(index, rings[message.ring].at[message.slot], core[index], 3, 1, 0)

    made = {tail: 0}
    pending = load(0)
    end = max(LAGS) + len(jobs)
    for tick in range(end + 1):
        if tick < len(jobs):
            following = load(tick + 1) if tick + 1 < len(jobs) else None
            for copy in pending:
                copy.wait()
            produce(tick)
            pending = following
            if jobs[tick].plane in (None, sizes[0] - 1):
                made.update({index: tick for index in jobs[tick].messages})
        for phase, lag in enumerate(LAGS):
            for index in sorted(made):
                if made[index] + lag == tick:
                    step(index, phase)
    for copy in sends:
        copy.wait_send()
    for copy in exchanges.values():
        copy.wait_send()


def weight_grads(devices, inputs, norm):
    sizes = grid_of(devices)
    names = list(inputs)
    at = {name: index for index, name in enumerate(names)}
    width = inputs["tokens"].shape[1]
    rows = width // devices
    patch_width = inputs["padded"].shape[1]
    hidden = inputs["hidden"].shape[1]
    planes = hidden // width
    third = width // 3
    outs = [(6, rows, width), (2, rows, patch_width), (planes * rows, width), (rows, hidden), (TILE_ROWS, LANES)]
    rings = [(2, rows, patch_width), (3, planes * rows, third), (2, rows, width)]
    jobs, messages = [], []

    def message(which, *rest):
        messages.append(Message(ORDERS[which], *rest))
        return len(messages) - 1

    for part in range(hidden // patch_width):
        start = part * patch_width
        index = message(part % 2, rows, patch_width, BF16, 3, (), start, 0, part % 2)
        jobs.append(Job(at["branch_three"], 0, at["hidden"], start, patch_width, (index,), None))
    ups = tuple(
        message((part + 1) % 2, planes * rows, third, BF16, 2, (), part * third, 1, part) for part in range(3)
    )
    for plane in range(sizes[0]):
        jobs.append(Job(at["grad_pre"], plane * width, at["second_low"], 0, width, ups, plane))
    for part, left in enumerate(("grad_keys", "grad_values")):
        index = message(part, rows, patch_width, BF16, 1, (part,), 0, 0, (part + 1) % 2)
        jobs.append(Job(at[left], 0, at["padded"], 0, patch_width, (index,), None))
    pairs = (
        ("branch_two", 0, "mixed_cross", 5),
        ("grad_cross", 0, "first_low", 4),
        ("branch_one", 0, "mixed_self", 3),
        ("grad_qkv", 0, "tokens", 0),
        ("grad_qkv", width, "tokens", 1),
        ("grad_qkv", 2 * width, "tokens", 2),
    )
    for part, (left, start, right, out) in enumerate(pairs):
        index = message(part % 2, rows, width, BF16, 0, (out,), 0, 2, part % 2)
        jobs.append(Job(at[left], start, at[right], 0, width, (index,), None))
    message(0, TILE_ROWS, LANES, F32, 4, (), 0, 0, 0)
    count = len(messages)

    def scratch(drop, lead):
        made = []
        for item in messages:
            gone = item.order[3 - drop : 3]
            outer = [sizes[gone[0]] - 1] if lead else []
            shape = (*outer, *[sizes[axis] for axis in range(3) if axis not in gone], item.rows, item.width)
            made.append(pltpu.VMEM(shape, item.dtype))
        return made

    slots = sum(sizes) - 3
    deep = max(array.shape[0] for array in inputs.values())
    return pl.pallas_call(
        functools.partial(products_kernel, sizes, tuple(jobs), tuple(messages), len(names), len(outs), len(rings)),
        in_specs=[pl.BlockSpec(memory_space=pl.ANY)] * (len(names) + 1),
        out_specs=[pl.BlockSpec(memory_space=pltpu.VMEM)] * len(outs),
        out_shape=[jax.ShapeDtypeStruct(shape, F32) for shape in outs],
        scratch_shapes=[
            *scratch(0, False),
            *scratch(0, False),
            *scratch(1, True),
            *scratch(2, True),
            *scratch(3, True),
            *[pltpu.VMEM((number, *sizes[:3], *shape), BF16) for number, *shape in rings],
            pltpu.VMEM((2, deep, width), BF16),
            pltpu.VMEM((2, deep, patch_width), BF16),
            pltpu.VMEM((width, patch_width), F32),
            pltpu.SemaphoreType.DMA((len(jobs), 2)),
            pltpu.SemaphoreType.DMA,
            pltpu.SemaphoreType.DMA((count, slots)),
            pltpu.SemaphoreType.DMA((count, slots)),
        ],
        compiler_params=pltpu.CompilerParams(collective_id=1, has_side_effects=True, vmem_limit_bytes=VMEM_BYTES),
        name="weight_grads",
    )(*inputs.values(), norm.reshape(*sizes, TILE_ROWS, LANES))


GATHER_ORDERS = {
    "query": 1,
    "key": 0,
    "value": 1,
    "out": 0,
    "cross_key": 1,
    "cross_value": 0,
    "cross_query": 1,
    "cross_out": 0,
    "up": 1,
    "down": 0,
}


def aligned(devices, shards):
    return devices % 32 == 0 and all(shard.shape[0] % TILE_ROWS == 0 for shard in shards.values())


def gather(devices, shards, norm):
    if not aligned(devices, shards):
        full = {name: lax.all_gather(shards[name], "dp", axis=0, tiled=True) for name in NAMES}
        return full, lax.all_gather(norm, "dp", axis=1, tiled=True)
    rows, width = norm.shape
    padded = jnp.zeros((1, TILE_ROWS, LANES), norm.dtype).at[0, :rows, :width].set(norm)
    blocks = [padded] + [shards[name][None] for name in GATHER_ORDERS]
    orders = [ORDERS[0]] + [ORDERS[at] for at in GATHER_ORDERS.values()]
    norms, *fulls = gather_all(blocks, orders, devices)
    norms = norms.reshape(devices, TILE_ROWS, LANES)[:, :rows, :width]
    norms = jnp.swapaxes(norms, 0, 1).reshape(rows, devices * width)
    return {name: array[0] for name, array in zip(GATHER_ORDERS, fulls)}, norms


def scatter(devices, shards, inputs, norm):
    width = inputs["tokens"].shape[1]
    if not aligned(devices, shards):
        products = (
            (inputs["grad_qkv"][:, :width], inputs["tokens"]),
            (inputs["grad_qkv"][:, width : 2 * width], inputs["tokens"]),
            (inputs["grad_qkv"][:, 2 * width :], inputs["tokens"]),
            (inputs["branch_one"], inputs["mixed_self"]),
            (inputs["grad_cross"], inputs["first_low"]),
            (inputs["grad_keys"], inputs["padded"]),
            (inputs["grad_values"], inputs["padded"]),
            (inputs["branch_two"], inputs["mixed_cross"]),
            (inputs["grad_pre"], inputs["second_low"]),
            (inputs["branch_three"], inputs["hidden"]),
        )
        sums = [tn(left, right).astype(BF16) for left, right in products]
        parts = [lax.psum_scatter(grad, "dp", scatter_dimension=0, tiled=True).astype(F32) for grad in sums]
        return parts, lax.psum_scatter(norm, "dp", scatter_dimension=1, tiled=True)
    rows = norm.shape[0]
    columns = norm.shape[1] // devices
    norm = jnp.swapaxes(norm.reshape(rows, devices, columns), 0, 1)
    padded = jnp.zeros((devices, TILE_ROWS, LANES), F32).at[:, :rows, :columns].set(norm)
    token, patch, up, down, norm = weight_grads(devices, inputs, padded)
    parts = [token[0], token[1], token[2], token[3], token[4], patch[0], patch[1], token[5], up, down]
    return parts, norm[:rows, :columns]


def local(devices, text, patches, segment_ids, row_image, *rest):
    *shards, norm_params, cotangent = rest
    shards = {name: jnp.swapaxes(shard, 0, 1) for name, shard in zip(NAMES, shards, strict=True)}
    rows, length, width = text.shape
    weights, norms = gather(devices, shards, norm_params)
    norms = norms.astype(F32)
    norms = jnp.concatenate([norms, jnp.zeros((2, width), F32)], axis=0)
    ids = segment_ids + 8 * jnp.arange(rows, dtype=jnp.int32)[:, None]
    padded, keys, values = image_rows(patches, weights["cross_key"], weights["cross_value"])
    (
        output,
        qkv,
        self_weights,
        mixed_self,
        normed_one,
        inverse_one,
        first_low,
        cross_low,
        cross_weights,
        mixed_cross,
        second_low,
        hidden,
        grad_pre,
        branch_three,
        grad_two,
        norm_late,
    ) = forward(
        row_image, text, ids, cotangent, keys, values, weights, norms, patches.shape[1]
    )
    (
        text_grad,
        branch_two,
        grad_cross,
        branch_one,
        grad_qkv,
        grad_keys,
        grad_values,
        norm_early,
    ) = backward(
        row_image,
        (grad_two, qkv, self_weights, normed_one, inverse_one, cross_low, cross_weights),
        keys,
        values,
        weights,
        norms,
        rows,
    )
    patch_grad = patch_grads(
        grad_keys, grad_values, weights["cross_key"], weights["cross_value"], patches.shape[1]
    )
    tokens = text.reshape(rows * length, width)
    patch_rows = padded.reshape(-1, padded.shape[-1])
    inputs = {
        "branch_three": branch_three,
        "hidden": hidden,
        "grad_pre": grad_pre,
        "second_low": second_low,
        "grad_keys": grad_keys.reshape(-1, width),
        "grad_values": grad_values.reshape(-1, width),
        "padded": patch_rows,
        "branch_two": branch_two,
        "mixed_cross": mixed_cross,
        "grad_cross": grad_cross,
        "first_low": first_low,
        "branch_one": branch_one,
        "mixed_self": mixed_self,
        "grad_qkv": grad_qkv,
        "tokens": tokens,
    }
    grads, norm_grad = scatter(devices, shards, inputs, (norm_late + norm_early)[:6])
    return (
        output.reshape(text.shape),
        text_grad.reshape(text.shape),
        patch_grad,
        *[jnp.swapaxes(grad, 0, 1) for grad in grads],
        norm_grad,
    )


def solution(mesh):
    split = P("dp", None, None)
    columns = P(None, "dp")
    in_specs = (split, split, P("dp", None), P("dp"), *([columns] * 11), split)
    out_specs = (split, split, split, *([columns] * 11))
    program = functools.partial(local, mesh.shape["dp"])
    return jax.shard_map(program, mesh=mesh, in_specs=in_specs, out_specs=out_specs, check_vma=False)
```
